32 devices in a mesh: grp: 4 (over y, core), seq: 8 (over z, x).
Axes of the slice: x: 2, y: 2, z: 4, core: 2. Of those that a mesh axis runs over, the one named last changes fastest.
Arguments:
- queries: bfloat16 [32768, 1024], P(('grp', 'seq')), may hold values from -6 to 6
- key_rows: bfloat16 [32768, 1024], P(('grp', 'seq')), may hold values from -6 to 6
- value_rows: bfloat16 [32768, 1024], P(('grp', 'seq')), may hold values from -6 to 6
- norm_gain: float32 [1024], replicated, may hold values from 0.25 to 1.75
- cotangent: bfloat16 [32768, 1024], P(('grp', 'seq')), may hold values from -6 to 6
Outputs:
- normed_out: bfloat16 [32768, 1024], P(('grp', 'seq'))
- grad_queries: bfloat16 [32768, 1024], P(('grp', 'seq'))
- grad_keys: bfloat16 [32768, 1024], P(('grp', 'seq'))
- grad_values: bfloat16 [32768, 1024], P(('grp', 'seq'))
The draws below stay inside these ranges and needn't reach their ends.
All inputs are finite; a program needn't handle non-finite values.
Results may differ from the reference program's by a relative error of at most 0.0058.
Values sent between devices are 32-bit elements; how exact they have to be, the bound alone decides.
No kernel may reach another device: no remote copies, remote signals or barrier semaphores. Data moves between devices by JAX's collectives and lax.ppermute only.
A program may use at most 128 MiB of HBM per device.

```python
import jax
import jax.numpy as jnp
from jax import lax

H = 8
HD = 128
BLOCK = 512
D = 1024
TOKENS = 32768


def levels(own_key, shape, pieces, least, largest):
    factor_of = 1.0
    for position, parts in pieces:
        draws = jax.random.uniform(jax.random.fold_in(jax.random.fold_in(own_key, 6), position), (parts,), jnp.float32, least / len(pieces), largest / len(pieces))
        factor_of = factor_of * jnp.repeat(jnp.exp(draws), shape[position] // parts).reshape((-1,) + (1,) * (len(shape) - 1 - position))
    return factor_of


def noise(key, dims, spread, reach, pieces=(), kind=jnp.bfloat16):
    drawn = jax.random.normal(key, dims, jnp.float32) * spread
    if len(pieces) > 0:
        drawn = levels(key, dims, pieces, -0.22, 0.18) * drawn
    return jnp.clip(drawn, min=-reach, max=reach).astype(kind)


def setup_inputs(seed: int = 0) -> dict:
    splits = jax.random.split(jax.random.key(seed), 6)
    queries = noise(splits[0], (TOKENS, D), 1.0, 6.0, ((0, 32),))
    key_rows = noise(splits[1], (TOKENS, D), 1.0, 6.0, ((0, 32),))
    value_rows = noise(splits[2], (TOKENS, D), 1.0, 6.0, ((0, 32),))
    norm_gain = jnp.clip(1.0 + 0.15 * jax.random.normal(splits[3], (D,), jnp.float32), 0.25, 1.75)
    cotangent = noise(splits[4], (TOKENS, D), 1.0, 6.0, ((0, 32),))
    return {"queries": queries, "key_rows": key_rows, "value_rows": value_rows, "norm_gain": norm_gain, "cotangent": cotangent}


EPSILON = 1e-06

def lower_mask(length):
    indices = jnp.arange(length)
    return indices[:, None] >= indices[None, :]

def round_half(value):
    return lax.optimization_barrier(value.astype(jnp.bfloat16)).astype(jnp.float32)

def reference(queries, key_rows, value_rows, norm_gain, cotangent):
    block_count = TOKENS // BLOCK
    features = H * HD
    block_shape = (block_count, BLOCK, H, HD)
    query_blocks = queries.reshape(block_shape)
    key_blocks = key_rows.reshape(block_shape)
    value_blocks = value_rows.reshape(block_shape)
    causal = lower_mask(BLOCK)[None]
    zero_state = jnp.zeros((H, HD, HD), jnp.float32)

    def forward_step(carry_state, inputs):
        query_blk, key_blk, value_blk = [member.astype(jnp.float32) for member in inputs]
        prior_state = round_half(carry_state)
        scores = jnp.einsum('thd,shd->hts', query_blk, key_blk)
        scores = round_half(jnp.where(causal, scores, 0.0))
        mixed_rows = jnp.einsum('hts,she->the', scores, value_blk)
        mixed_rows = mixed_rows + jnp.einsum('thd,hde->the', query_blk, prior_state)
        carry_state = carry_state + jnp.einsum('shd,she->hde', key_blk, value_blk)
        return (carry_state, (mixed_rows, prior_state))
    final_state, (attended, priors) = lax.scan(forward_step, zero_state, (query_blocks, key_blocks, value_blocks))
    attended = attended.reshape(TOKENS, features)
    inverse = lax.rsqrt(lax.optimization_barrier(jnp.mean(attended * attended, axis=1, keepdims=True)) + EPSILON)
    unit_rows = attended * inverse
    gain_rows = norm_gain.astype(jnp.float32)[None, :]
    normed_out = (unit_rows * gain_rows).astype(jnp.bfloat16)
    scaled = cotangent.astype(jnp.float32) * gain_rows
    grad_attended = inverse * (scaled - unit_rows * lax.optimization_barrier(jnp.mean(scaled * unit_rows, axis=1, keepdims=True)))
    grad_blocks = grad_attended.astype(jnp.bfloat16).reshape(block_shape)

    def backward_step(carry_state, inputs):
        query_blk, key_blk, value_blk, grad_blk = [member.astype(jnp.float32) for member in inputs[:4]]
        prior_state = inputs[4]
        later_state = round_half(carry_state)
        scores = jnp.einsum('thd,shd->hts', query_blk, key_blk)
        scores = round_half(jnp.where(causal, scores, 0.0))
        grad_scores = jnp.einsum('the,she->hts', grad_blk, value_blk)
        grad_scores = round_half(jnp.where(causal, grad_scores, 0.0))
        grad_q = jnp.einsum('hts,shd->thd', grad_scores, key_blk) + jnp.einsum('the,hde->thd', grad_blk, prior_state)
        grad_k = jnp.einsum('hts,thd->shd', grad_scores, query_blk) + jnp.einsum('she,hde->shd', value_blk, later_state)
        grad_v = jnp.einsum('hts,the->she', scores, grad_blk) + jnp.einsum('shd,hde->she', key_blk, later_state)
        carry_state = carry_state + jnp.einsum('thd,the->hde', query_blk, grad_blk)
        return (carry_state, (grad_q.astype(jnp.bfloat16), grad_k.astype(jnp.bfloat16), grad_v.astype(jnp.bfloat16)))
    final_grad, (grad_q, grad_k, grad_v) = lax.scan(backward_step, zero_state, (query_blocks, key_blocks, value_blocks, grad_blocks, priors), reverse=True)
    return (normed_out, grad_q.reshape(TOKENS, features), grad_k.reshape(TOKENS, features), grad_v.reshape(TOKENS, features))
```

```python
import functools

import jax
import jax.numpy as jnp
from jax import lax
from jax.experimental import pallas as pl
from jax.experimental.pallas import tpu as pltpu
from jax.sharding import PartitionSpec as P

H = 8
HD = 128
BLOCK = 512
EPSILON = 1e-06
AXES = ("grp", "seq")
LANES = 2
QUAD = 4
SHARE = H // (LANES * QUAD)
TILE = 256
F32 = jnp.float32
BF16 = jnp.bfloat16


def mm(a, b, ca, cb):
    return lax.dot_general(a, b, (((ca,), (cb,)), ((), ())), preferred_element_type=F32)


def place_of(head, where):
    unit = head // SHARE
    lane = (unit // QUAD) ^ where[0]
    slot = (unit % QUAD) ^ where[1]
    return slot, lane, head % SHARE


def put_piece(pieces, head, where, value):
    slot, lane, share = place_of(head, where)
    for i, piece in enumerate(pieces):

        @pl.when(slot == i)
        def _():
            piece[lane, share] = value


def piece_shapes():
    return [jax.ShapeDtypeStruct((LANES, SHARE, HD, HD), F32)] * QUAD


def whole(shape):
    return pl.BlockSpec(shape, lambda *_: (0,) * len(shape))


def totals_kernel(where, k_ref, v_ref, *outs):
    pieces, inside = outs[:QUAD], outs[QUAD]
    head = pl.program_id(0)
    blocks = k_ref.shape[0] // BLOCK
    total = None
    for b in range(blocks):
        rows = pl.ds(b * BLOCK, BLOCK)
        state = mm(k_ref[rows, :], v_ref[rows, :], 0, 0)
        inside[b, 0] = jnp.zeros_like(state) if total is None else total
        total = state if total is None else total + state
    put_piece(pieces, head, where, total)


def totals(where, keys, values):
    tokens = keys.shape[0]
    blocks = tokens // BLOCK
    column = pl.BlockSpec((tokens, HD), lambda h, *_: (0, h))
    piece = (LANES, SHARE, HD, HD)
    return pl.pallas_call(
        totals_kernel,
        out_shape=piece_shapes() + [jax.ShapeDtypeStruct((blocks, H, HD, HD), F32)],
        grid_spec=pltpu.PrefetchScalarGridSpec(
            num_scalar_prefetch=1,
            grid=(H,),
            in_specs=[column, column],
            out_specs=[whole(piece)] * QUAD
            + [pl.BlockSpec((blocks, 1, HD, HD), lambda h, *_: (0, h, 0, 0))],
        ),
        cost_estimate=pl.CostEstimate(
            flops=2 * tokens * H * HD * HD, bytes_accessed=4 * tokens * H * HD, transcendentals=0
        ),
        name="totals",
    )(where, keys, values)


def triangle(upper=False):
    row = lax.broadcasted_iota(jnp.int32, (TILE, TILE), 0)
    col = lax.broadcasted_iota(jnp.int32, (TILE, TILE), 1)
    return row <= col if upper else row >= col


def local_kernel(q_ref, k_ref, v_ref, out_ref):
    mask = triangle()
    for i in range(BLOCK // TILE):
        rows = pl.ds(i * TILE, TILE)
        q = q_ref[rows, :]
        diag = jnp.where(mask, mm(q, k_ref[rows, :], 1, 1), 0.0).astype(BF16)
        acc = mm(diag, v_ref[rows, :], 1, 0)
        if i:
            past = pl.ds(0, i * TILE)
            acc += mm(mm(q, k_ref[past, :], 1, 1).astype(BF16), v_ref[past, :], 1, 0)
        out_ref[rows, :] = acc


def local_part(queries, keys, values):
    tokens = queries.shape[0]
    blk = pl.BlockSpec((BLOCK, HD), lambda h, b: (b, h))
    return pl.pallas_call(
        local_kernel,
        out_shape=jax.ShapeDtypeStruct(queries.shape, F32),
        grid=(H, tokens // BLOCK),
        in_specs=[blk] * 3,
        out_specs=blk,
        cost_estimate=pl.CostEstimate(
            flops=4 * tokens * BLOCK * H * HD, bytes_accessed=10 * tokens * H * HD, transcendentals=0
        ),
        name="local",
    )(queries, keys, values)


def middle_kernel(where, local_ref, q_ref, dy_ref, gain_ref, *refs):
    carried, inside = refs[:QUAD], refs[QUAD]
    out_ref, grad_ref, prior_ref = refs[QUAD + 1 : QUAD + 4]
    pieces, later_ref = refs[QUAD + 4 : 2 * QUAD + 4], refs[2 * QUAD + 4]
    att_ref, run_ref = refs[2 * QUAD + 5 :]
    step = pl.program_id(0)
    steps = pl.num_programs(0)
    per_block = BLOCK // q_ref.shape[0]
    block = steps // per_block - 1 - step // per_block

    @pl.when(step % per_block == 0)
    def _():
        for head in range(H):
            slot, lane, share = place_of(head, where)
            for i in range(QUAD):

                @pl.when(slot == i)
                def _():
                    prior_ref[0, head] = (carried[i][lane, share] + inside[0, head]).astype(BF16)

    @pl.when(step == 0)
    def _():
        run_ref[...] = jnp.zeros_like(run_ref)

    @pl.when(step % per_block == 0)
    def _():
        later_ref[0] = run_ref[...]

    square = None
    for head in range(H):
        cols = pl.ds(head * HD, HD)
        att = local_ref[:, cols] + mm(q_ref[:, cols], prior_ref[0, head], 1, 0)
        att_ref[:, cols] = att
        square = att * att if square is None else square + att * att
    features = H * HD
    inverse = lax.rsqrt(jnp.sum(square, axis=1, keepdims=True) / features + EPSILON)
    cross = None
    for head in range(H):
        cols = pl.ds(head * HD, HD)
        unit = att_ref[:, cols] * inverse
        gain = gain_ref[:, cols]
        out_ref[:, cols] = (unit * gain).astype(BF16)
        term = dy_ref[:, cols].astype(F32) * gain * unit
        cross = term if cross is None else cross + term
    mean = jnp.sum(cross, axis=1, keepdims=True) / features
    for head in range(H):
        cols = pl.ds(head * HD, HD)
        unit = att_ref[:, cols] * inverse
        scaled = dy_ref[:, cols].astype(F32) * gain_ref[:, cols]
        grad = (inverse * (scaled - unit * mean)).astype(BF16)
        grad_ref[:, cols] = grad
        run_ref[head] += mm(q_ref[:, cols], grad, 0, 0)

    @pl.when(step == steps - 1)
    def _():
        for head in range(H):
            put_piece(pieces, head, where, run_ref[head])


def middle(where, local, queries, cotangent, gain, carried, inside):
    tokens, features = queries.shape
    rows = TILE
    per_block = BLOCK // rows
    blocks = tokens // BLOCK
    steps = tokens // rows

    def row_of(i, *_):
        return ((blocks - 1 - i // per_block) * per_block + i % per_block, 0)

    def block_of(i, *_):
        return (blocks - 1 - i // per_block, 0, 0, 0)

    tile = pl.BlockSpec((rows, features), row_of)
    state = pl.BlockSpec((1, H, HD, HD), block_of)
    piece = (LANES, SHARE, HD, HD)
    return pl.pallas_call(
        middle_kernel,
        out_shape=[
            jax.ShapeDtypeStruct((tokens, features), BF16),
            jax.ShapeDtypeStruct((tokens, features), BF16),
            jax.ShapeDtypeStruct((blocks, H, HD, HD), BF16),
        ]
        + piece_shapes()
        + [jax.ShapeDtypeStruct((blocks, H, HD, HD), F32)],
        grid_spec=pltpu.PrefetchScalarGridSpec(
            num_scalar_prefetch=1,
            grid=(steps,),
            in_specs=[tile, tile, tile, whole((1, features))] + [whole(piece)] * QUAD + [state],
            out_specs=[tile, tile, state] + [whole(piece)] * QUAD + [state],
            scratch_shapes=[pltpu.VMEM((rows, features), F32), pltpu.VMEM((H, HD, HD), F32)],
        ),
        cost_estimate=pl.CostEstimate(
            flops=4 * tokens * features * HD, bytes_accessed=12 * tokens * features, transcendentals=0
        ),
        name="middle",
    )(where, local, queries, cotangent, gain, *carried, inside)


def back_kernel(q_ref, k_ref, v_ref, g_ref, prior_ref, gq_ref, lk_ref, lv_ref):
    mask = triangle()
    turned = triangle(True)
    tiles = BLOCK // TILE
    prior = prior_ref[0, 0]
    for i in range(tiles):
        rows = pl.ds(i * TILE, TILE)
        q, k, v, g = q_ref[rows, :], k_ref[rows, :], v_ref[rows, :], g_ref[rows, :]
        acc = mm(g, prior, 1, 1)
        acc += mm(jnp.where(mask, mm(g, v, 1, 1), 0.0).astype(BF16), k, 1, 0)
        if i:
            past = pl.ds(0, i * TILE)
            acc += mm(mm(g, v_ref[past, :], 1, 1).astype(BF16), k_ref[past, :], 1, 0)
        gq_ref[rows, :] = acc.astype(BF16)
        lk = mm(jnp.where(turned, mm(v, g, 1, 1), 0.0).astype(BF16), q, 1, 0)
        lv = mm(jnp.where(turned, mm(k, q, 1, 1), 0.0).astype(BF16), g, 1, 0)
        if i < tiles - 1:
            rest = pl.ds((i + 1) * TILE, BLOCK - (i + 1) * TILE)
            lk += mm(mm(v, g_ref[rest, :], 1, 1).astype(BF16), q_ref[rest, :], 1, 0)
            lv += mm(mm(k, q_ref[rest, :], 1, 1).astype(BF16), g_ref[rest, :], 1, 0)
        lk_ref[rows, :] = lk
        lv_ref[rows, :] = lv


def back_part(queries, keys, values, grads, prior):
    tokens = queries.shape[0]
    blk = pl.BlockSpec((BLOCK, HD), lambda h, b: (b, h))
    return pl.pallas_call(
        back_kernel,
        out_shape=[
            jax.ShapeDtypeStruct(queries.shape, BF16),
            jax.ShapeDtypeStruct(queries.shape, F32),
            jax.ShapeDtypeStruct(queries.shape, F32),
        ],
        grid=(H, tokens // BLOCK),
        in_specs=[blk] * 4 + [pl.BlockSpec((1, 1, HD, HD), lambda h, b: (b, h, 0, 0))],
        out_specs=[blk] * 3,
        cost_estimate=pl.CostEstimate(
            flops=12 * tokens * BLOCK * H * HD, bytes_accessed=18 * tokens * H * HD, transcendentals=0
        ),
        name="back",
    )(queries, keys, values, grads, prior)


def final_kernel(where, lk_ref, lv_ref, k_ref, v_ref, *refs):
    carried, later = refs[:QUAD], refs[QUAD]
    gk_ref, gv_ref, state_ref = refs[QUAD + 1 :]
    head = pl.program_id(0)
    slot, lane, share = place_of(head, where)
    for i in range(QUAD):

        @pl.when(slot == i)
        def _():
            state_ref[...] = carried[i][lane, share]

    for b in range(k_ref.shape[0] // BLOCK):
        rows = pl.ds(b * BLOCK, BLOCK)
        state = (state_ref[...] + later[b, 0]).astype(BF16)
        gk_ref[rows, :] = (lk_ref[rows, :] + mm(v_ref[rows, :], state, 1, 1)).astype(BF16)
        gv_ref[rows, :] = (lv_ref[rows, :] + mm(k_ref[rows, :], state, 1, 0)).astype(BF16)


def final_part(where, local_k, local_v, keys, values, carried, later):
    tokens, features = keys.shape
    blocks = tokens // BLOCK
    column = pl.BlockSpec((tokens, HD), lambda h, *_: (0, h))
    piece = (LANES, SHARE, HD, HD)
    return pl.pallas_call(
        final_kernel,
        out_shape=[jax.ShapeDtypeStruct((tokens, features), BF16)] * 2,
        grid_spec=pltpu.PrefetchScalarGridSpec(
            num_scalar_prefetch=1,
            grid=(H,),
            in_specs=[column] * 4
            + [whole(piece)] * QUAD
            + [pl.BlockSpec((blocks, 1, HD, HD), lambda h, *_: (0, h, 0, 0))],
            out_specs=[column] * 2,
            scratch_shapes=[pltpu.VMEM((HD, HD), F32)],
        ),
        cost_estimate=pl.CostEstimate(
            flops=4 * tokens * features * HD, bytes_accessed=16 * tokens * features, transcendentals=0
        ),
        name="final",
    )(where, local_k, local_v, keys, values, *carried, later)


def moved(value, move):
    groups, shards = lax.axis_size("grp"), lax.axis_size("seq")
    pairs = []
    for g in range(groups):
        for s in range(shards):
            to_g, to_s = move(g, s)
            pairs.append((g * shards + s, to_g * shards + to_s))
    return lax.ppermute(value, AXES, pairs)


def carry(pieces, reverse):
    grp, seq = lax.axis_index("grp"), lax.axis_index("seq")
    lane, quad = grp % LANES, seq % QUAD
    row, far = grp // LANES, seq // QUAD
    row_count = lax.axis_size("grp") // LANES
    far_count = lax.axis_size("seq") // QUAD
    order = (3, 1, 2)

    def before(a, b):
        return a > b if reverse else a < b

    def swap_quad(o):
        return lambda g, s: (g, s ^ o)

    def swap_lane(g, s):
        return g ^ 1, s

    def shift(dr, df):
        return lambda g, s: (
            (g // LANES + dr) % row_count * LANES + g % LANES,
            (s // QUAD + df) % far_count * QUAD + s % QUAD,
        )

    held = [pieces[0]] + [None] * (QUAD - 1)
    for o in order:
        held[o] = moved(pieces[o], swap_quad(o))
    quad_sum = held[0] + held[1] + held[2] + held[3]
    mine, other = quad_sum[0], moved(quad_sum[1], swap_lane)
    pair, both = jnp.stack([mine, other]), mine + other
    shifts = [(dr, df) for dr in range(row_count) for df in range(far_count) if dr or df]
    shifts.sort(key=lambda shift_by: -sum(shift_by))
    came = [moved(both if dr else pair, shift(dr, df)) for dr, df in shifts]
    takes = lane == (0 if reverse else 1)
    sum_mine = jnp.where(takes, other, 0.0)
    sum_other = jnp.where(takes, 0.0, mine)
    for (dr, df), value in zip(shifts, came):
        if dr:
            value = jnp.where(before((row - dr) % row_count, row), value, 0.0)
            sum_mine, sum_other = sum_mine + value, sum_other + value
        else:
            near = before((far - df) % far_count, far)
            sum_mine += jnp.where(near, value[0], 0.0) + jnp.where(takes, value[1], 0.0)
            sum_other += jnp.where(near, value[1], 0.0) + jnp.where(takes, 0.0, value[0])
    base = jnp.stack([sum_mine, moved(sum_other, swap_lane)])
    back = []
    for o in range(QUAD):
        value = base
        for i in range(QUAD):
            if i != o:
                value = value + jnp.where(before(quad ^ i, quad ^ o), held[i], 0.0)
        back.append(value)
    result = [back[0]] + [None] * (QUAD - 1)
    for o in order:
        result[o] = moved(back[o], swap_quad(o))
    return result


def body(queries, key_rows, value_rows, norm_gain, cotangent):
    grp, seq = lax.axis_index("grp"), lax.axis_index("seq")
    where = jnp.stack([grp % LANES, seq % QUAD]).astype(jnp.int32)
    *pieces, inside = totals(where, key_rows, value_rows)
    local = local_part(queries, key_rows, value_rows)
    prior = carry(pieces, False)
    normed, grads, prior_half, *rest = middle(
        where, local, queries, cotangent, norm_gain[None, :], prior, inside
    )
    grad_pieces, later = rest[:QUAD], rest[QUAD]
    grad_q, local_k, local_v = back_part(queries, key_rows, value_rows, grads, prior_half)
    after = carry(grad_pieces, True)
    grad_k, grad_v = final_part(where, local_k, local_v, key_rows, value_rows, after, later)
    return normed, grad_q, grad_k, grad_v


def solution(mesh):
    rows = P(AXES, None)
    return jax.shard_map(
        body,
        mesh=mesh,
        in_specs=(rows, rows, rows, P(), rows),
        out_specs=(rows, rows, rows, rows),
        check_vma=False,
    )
```

```python
import functools

import jax
import jax.numpy as jnp
from jax import lax
from jax.experimental import pallas as pl
from jax.experimental.pallas import tpu as pltpu
from jax.sharding import PartitionSpec as P


H = 8
HD = 128
BLOCK = 512
EPSILON = 1e-06
AXES = ("grp", "seq")
LANES = 2
QUAD = 4
SHARE = H // (LANES * QUAD)
TILE = 256
CUT = 512
SLAB = 256
UNROLL_TOTALS = 4
UNROLL_LOCAL = 4
UNROLL_BACK = 4
UNROLL_FINAL = 4
DEPTH = 2
F32 = jnp.float32
BF16 = jnp.bfloat16


def mm(a, b, ca, cb):
    return lax.dot_general(a, b, (((ca,), (cb,)), ((), ())), preferred_element_type=F32)


def place_of(head, where):
    unit = head // SHARE
    lane = (unit // QUAD) ^ where[0]
    slot = (unit % QUAD) ^ where[1]
    return slot, lane, head % SHARE


def put_piece(pieces, head, where, value):
    slot, lane, share = place_of(head, where)
    for i, piece in enumerate(pieces):

        @pl.when(slot == i)
        def _():
            piece[lane, share] = value


def vmem(*shape, dtype=F32):
    return pltpu.VMEM(shape, dtype)


def near(value):
    return pltpu.with_memory_space_constraint(value, pltpu.VMEM)


def far(value):
    return pltpu.with_memory_space_constraint(value, pltpu.HBM)


def piece_shapes():
    return [vmem(LANES, SHARE, HD, HD)] * QUAD


def call(kernel, out_shape, args, flops, scratch=(), grant=8, far_in=(), far_out=()):
    any_space = pl.BlockSpec(memory_space=pltpu.HBM)
    near_space = pl.BlockSpec(memory_space=pltpu.VMEM)
    in_specs = [pl.BlockSpec(memory_space=pltpu.SMEM)]
    in_specs += [any_space if i in far_in else near_space for i in range(len(args) - 1)]
    out_specs = [any_space if i in far_out else near_space for i in range(len(out_shape))]
    args = [args[0]] + [far(a) if i in far_in else near(a) for i, a in enumerate(args[1:])]
    return pl.pallas_call(
        kernel,
        out_shape=out_shape,
        in_specs=in_specs,
        out_specs=out_specs,
        scratch_shapes=scratch,
        compiler_params=pltpu.CompilerParams(vmem_limit_bytes=grant << 20),
        cost_estimate=pl.CostEstimate(flops=flops, bytes_accessed=flops // 100, transcendentals=0),
    )(*args)


def head_cols(head):
    return pl.ds(pl.multiple_of(head * HD, HD), HD)


def over_heads(step, unroll):
    def several(i, _):
        for j in range(unroll):
            step(i * unroll + j)
        return 0

    lax.fori_loop(0, H // unroll, several, 0)


def totals_kernel(where, k_far, v_far, *refs):
    pieces, (inside, k_ref, v_ref, run, sems) = refs[:QUAD], refs[QUAD:]
    blocks = k_ref.shape[0] // BLOCK
    copies = []
    for b in range(blocks):
        rows = pl.ds(b * BLOCK, BLOCK)
        for j, (source, target) in enumerate(((k_far, k_ref), (v_far, v_ref))):
            copies.append(pltpu.make_async_copy(source.at[rows, :], target.at[rows, :], sems.at[b, j]))
    for copy in copies[: 2 * DEPTH]:
        copy.start()
    for b in range(blocks):
        for j in range(2):
            copies[2 * b + j].wait()
            if b + DEPTH < blocks:
                copies[2 * (b + DEPTH) + j].start()
        rows = pl.ds(b * BLOCK, BLOCK)
        for head in range(H):
            cols = pl.ds(head * HD, HD)
            state = mm(k_ref[rows, cols], v_ref[rows, cols], 0, 0)
            inside[b, head] = run[head] if b else jnp.zeros_like(state)
            state = run[head] + state if b else state
            if b < blocks - 1:
                run[head] = state
            else:
                put_piece(pieces, head, where, state)


def totals(where, keys, values):
    tokens, features = keys.shape
    blocks = tokens // BLOCK
    return call(
        totals_kernel,
        piece_shapes()
        + [vmem(blocks, H, HD, HD)]
        + [vmem(tokens, features, dtype=BF16)] * 2,
        [where, keys, values],
        2 * tokens * features * HD,
        scratch=[vmem(H, HD, HD), pltpu.SemaphoreType.DMA((blocks, 2))],
        far_in=(0, 1),
    )


def triangle(size, upper=False):
    row = lax.broadcasted_iota(jnp.int32, (size, size), 0)
    col = lax.broadcasted_iota(jnp.int32, (size, size), 1)
    return row <= col if upper else row >= col


def local_kernel(where, q_ref, k_ref, v_ref, out_ref):
    mask = triangle(CUT)

    def step(unit):
        block, cols = unit // H, head_cols(unit % H)
        for i in range(BLOCK // CUT):
            rows = pl.ds(pl.multiple_of(block * BLOCK + i * CUT, CUT), CUT)
            q = q_ref[rows, cols]
            diag = jnp.where(mask, mm(q, k_ref[rows, cols], 1, 1), 0.0).astype(BF16)
            acc = mm(diag, v_ref[rows, cols], 1, 0)
            if i:
                past = pl.ds(pl.multiple_of(block * BLOCK, CUT), i * CUT)
                acc += mm(mm(q, k_ref[past, cols], 1, 1).astype(BF16), v_ref[past, cols], 1, 0)
            out_ref[rows, cols] = acc

    def several(i, _):
        for j in range(UNROLL_LOCAL):
            step(i * UNROLL_LOCAL + j)
        return 0

    lax.fori_loop(0, q_ref.shape[0] // BLOCK * H // UNROLL_LOCAL, several, 0)


def local_part(where, queries, keys, values):
    tokens, features = queries.shape
    return call(
        local_kernel,
        [vmem(tokens, features)],
        [where, queries, keys, values],
        4 * tokens * BLOCK * features,
    )[0]


def middle_kernel(where, local_ref, q_ref, dy_ref, gain_ref, *refs):
    carried, inside = refs[:QUAD], refs[QUAD]
    out_ref, grad_ref, prior_ref = refs[QUAD + 1 : QUAD + 4]
    pieces, later_ref = refs[QUAD + 4 : 2 * QUAD + 4], refs[2 * QUAD + 4]
    att_ref, run_ref = refs[2 * QUAD + 5 :]
    blocks = q_ref.shape[0] // BLOCK
    features = H * HD
    for head in range(H):
        slot, lane, share = place_of(head, where)
        for i in range(QUAD):

            @pl.when(slot == i)
            def _():
                for b in range(blocks):
                    prior_ref[b, head] = (carried[i][lane, share] + inside[b, head]).astype(BF16)

    run_ref[...] = jnp.zeros_like(run_ref)

    def tile_step(block, i):
        rows = pl.ds(pl.multiple_of(block * BLOCK + i * SLAB, SLAB), SLAB)
        square = None
        for head in range(H):
            cols = pl.ds(head * HD, HD)
            att = local_ref[rows, cols] + mm(q_ref[rows, cols], prior_ref[block, head], 1, 0)
            att_ref[:, cols] = att
            square = att * att if square is None else square + att * att
        inverse = lax.rsqrt(jnp.sum(square, axis=1, keepdims=True) / features + EPSILON)
        cross = None
        for head in range(H):
            cols = pl.ds(head * HD, HD)
            unit = att_ref[:, cols] * inverse
            gain = gain_ref[:, cols]
            out_ref[rows, cols] = (unit * gain).astype(BF16)
            term = dy_ref[rows, cols].astype(F32) * gain * unit
            cross = term if cross is None else cross + term
        mean = jnp.sum(cross, axis=1, keepdims=True) / features
        for head in range(H):
            cols = pl.ds(head * HD, HD)
            unit = att_ref[:, cols] * inverse
            scaled = dy_ref[rows, cols].astype(F32) * gain_ref[:, cols]
            grad_ref[rows, cols] = (inverse * (scaled - unit * mean)).astype(BF16)

    for block in reversed(range(blocks)):
        rows = pl.ds(block * BLOCK, BLOCK)
        lax.fori_loop(0, BLOCK // SLAB, lambda i, _: tile_step(block, i) or 0, 0)
        later_ref[block] = run_ref[...]

        def add(head):
            cols = head_cols(head)
            run_ref[head] += mm(q_ref[rows, cols], grad_ref[rows, cols], 0, 0)

        over_heads(add, UNROLL_TOTALS)
    for head in range(H):
        put_piece(pieces, head, where, run_ref[head])


def middle(where, local, queries, cotangent, gain, carried, inside):
    tokens, features = queries.shape
    blocks = tokens // BLOCK
    return call(
        middle_kernel,
        [vmem(tokens, features, dtype=BF16)] * 2
        + [vmem(blocks, H, HD, HD, dtype=BF16)]
        + piece_shapes()
        + [vmem(blocks, H, HD, HD)],
        [where, local, queries, cotangent, gain, *carried, inside],
        4 * tokens * features * HD,
        scratch=[vmem(SLAB, features), vmem(H, HD, HD)],
    )


def over_units(count, step):
    def several(i, _):
        for j in range(UNROLL_BACK):
            unit = i * UNROLL_BACK + j
            step(unit // H, unit % H)
        return 0

    lax.fori_loop(0, count // UNROLL_BACK, several, 0)


def block_part(block, first, count):
    return pl.ds(pl.multiple_of(block * BLOCK + first * CUT, CUT), count * CUT)


def query_kernel(where, g_ref, v_ref, k_ref, prior_ref, out_ref):
    mask = triangle(CUT)

    def step(block, head):
        cols = head_cols(head)
        for i in range(BLOCK // CUT):
            rows = block_part(block, i, 1)
            g = g_ref[rows, cols]
            acc = mm(g, prior_ref[block, head], 1, 1)
            scores = jnp.where(mask, mm(g, v_ref[rows, cols], 1, 1), 0.0).astype(BF16)
            acc += mm(scores, k_ref[rows, cols], 1, 0)
            if i:
                past = block_part(block, 0, i)
                scores = mm(g, v_ref[past, cols], 1, 1).astype(BF16)
                acc += mm(scores, k_ref[past, cols], 1, 0)
            out_ref[rows, cols] = acc.astype(BF16)

    over_units(g_ref.shape[0] // BLOCK * H, step)


def query_part(where, grads, values, keys, prior):
    tokens, features = grads.shape
    return call(
        query_kernel,
        [vmem(tokens, features, dtype=BF16)],
        [where, grads, values, keys, prior],
        4 * tokens * BLOCK * features,
    )[0]


def turned_kernel(where, a_ref, b_ref, c_ref, ready_ref, out_ref, far_ref, sem):
    copy = pltpu.make_async_copy(ready_ref, far_ref, sem)
    copy.start()
    mask, tiles = triangle(CUT, True), BLOCK // CUT

    def step(block, head):
        cols = head_cols(head)
        for i in range(tiles):
            rows = block_part(block, i, 1)
            a = a_ref[rows, cols]
            scores = jnp.where(mask, mm(a, b_ref[rows, cols], 1, 1), 0.0).astype(BF16)
            acc = mm(scores, c_ref[rows, cols], 1, 0)
            if i < tiles - 1:
                rest = block_part(block, i + 1, tiles - 1 - i)
                scores = mm(a, b_ref[rest, cols], 1, 1).astype(BF16)
                acc += mm(scores, c_ref[rest, cols], 1, 0)
            out_ref[rows, cols] = acc

    over_units(a_ref.shape[0] // BLOCK * H, step)
    copy.wait()


def turned_part(where, a, b, c, ready):
    tokens, features = a.shape
    return call(
        turned_kernel,
        [vmem(tokens, features), jax.ShapeDtypeStruct(ready.shape, ready.dtype)],
        [where, a, b, c, ready],
        4 * tokens * BLOCK * features,
        scratch=[pltpu.SemaphoreType.DMA(())],
        far_out=(1,),
    )


def final_kernel(where, lk_ref, lv_ref, k_ref, v_ref, *refs):
    carried, later = refs[:QUAD], refs[QUAD]
    gk_far, gv_far, gk_ref, gv_ref, state_ref, sems = refs[QUAD + 1 :]
    blocks = k_ref.shape[0] // BLOCK
    for head in range(H):
        slot, lane, share = place_of(head, where)
        for i in range(QUAD):

            @pl.when(slot == i)
            def _():
                for b in range(blocks):
                    state_ref[b, head] = (carried[i][lane, share] + later[b, head]).astype(BF16)

    copies = []
    for i in range(k_ref.shape[0] // TILE):
        rows = pl.ds(i * TILE, TILE)
        block = i // (BLOCK // TILE)

        def one(head):
            cols = head_cols(head)
            state = state_ref[block, head]
            gk_ref[rows, cols] = (lk_ref[rows, cols] + mm(v_ref[rows, cols], state, 1, 1)).astype(BF16)
            gv_ref[rows, cols] = (lv_ref[rows, cols] + mm(k_ref[rows, cols], state, 1, 0)).astype(BF16)

        over_heads(one, UNROLL_FINAL)
        for j, (source, target) in enumerate(((gk_ref, gk_far), (gv_ref, gv_far))):
            copy = pltpu.make_async_copy(source.at[rows, :], target.at[rows, :], sems.at[i, j])
            copy.start()
            copies.append(copy)
    for copy in copies:
        copy.wait()


def final_part(where, local_k, local_v, keys, values, carried, later):
    tokens, features = keys.shape
    blocks = tokens // BLOCK
    return call(
        final_kernel,
        [jax.ShapeDtypeStruct((tokens, features), BF16)] * 2,
        [where, local_k, local_v, keys, values, *carried, later],
        4 * tokens * features * HD,
        scratch=[
            vmem(tokens, features, dtype=BF16),
            vmem(tokens, features, dtype=BF16),
            vmem(blocks, H, HD, HD, dtype=BF16),
            pltpu.SemaphoreType.DMA((tokens // TILE, 2)),
        ],
        far_out=(0, 1),
        grant=12,
    )


def moved(value, move):
    groups, shards = lax.axis_size("grp"), lax.axis_size("seq")
    pairs = []
    for g in range(groups):
        for s in range(shards):
            to_g, to_s = move(g, s)
            pairs.append((g * shards + s, to_g * shards + to_s))
    return lax.ppermute(value, AXES, pairs)


def sum_kernel(where, *refs):
    held, (mine_ref, rest_ref) = refs[:QUAD], refs[QUAD:]
    for lane, out in enumerate((mine_ref, rest_ref)):
        out[...] = (held[0][lane] + held[1][lane]) + (held[2][lane] + held[3][lane])


def pair_kernel(where, mine_ref, other_ref, pair_ref, both_ref):
    mine, other = mine_ref[...], other_ref[...]
    pair_ref[0], pair_ref[1] = mine, other
    both_ref[...] = mine + other


def before(a, b, reverse):
    return a > b if reverse else a < b


def base_kernel(shifts, counts, reverse, where, pair_ref, *refs):
    came, (mine_ref, other_ref) = refs[: len(shifts)], refs[len(shifts) :]
    lane, row, far = where[0], where[2], where[3]
    takes = lane == (0 if reverse else 1)
    mine, other = pair_ref[0], pair_ref[1]
    sum_mine, sum_other = jnp.where(takes, other, 0.0), jnp.where(takes, 0.0, mine)
    for (dr, df), value in zip(shifts, came):
        if dr:
            source = lax.rem(row - dr + counts[0], counts[0])
            add = jnp.where(before(source, row, reverse), value[...], 0.0)
            sum_mine, sum_other = sum_mine + add, sum_other + add
        else:
            near_by = before(lax.rem(far - df + counts[1], counts[1]), far, reverse)
            mine, other = value[0], value[1]
            sum_mine += jnp.where(near_by, mine, 0.0) + jnp.where(takes, other, 0.0)
            sum_other += jnp.where(near_by, other, 0.0) + jnp.where(takes, 0.0, mine)
    mine_ref[...], other_ref[...] = sum_mine, sum_other


def back_sum_kernel(reverse, where, mine_ref, other_ref, *refs):
    held, back = refs[:QUAD], refs[QUAD:]
    quad = where[1]
    for lane, base in enumerate((mine_ref, other_ref)):
        for o in range(QUAD):
            value = base[...]
            for i in range(QUAD):
                if i != o:
                    near_by = before(quad ^ i, quad ^ o, reverse)
                    value += jnp.where(near_by, held[i][lane], 0.0)
            back[o][lane] = value


def carry(where, pieces, reverse):
    counts = lax.axis_size("grp") // LANES, lax.axis_size("seq") // QUAD
    order = (3, 1, 2)
    one, two = vmem(SHARE, HD, HD), vmem(LANES, SHARE, HD, HD)

    def swap_quad(o):
        return lambda g, s: (g, s ^ o)

    def swap_lane(g, s):
        return g ^ 1, s

    def shift(dr, df):
        return lambda g, s: (
            (g // LANES + dr) % counts[0] * LANES + g % LANES,
            (s // QUAD + df) % counts[1] * QUAD + s % QUAD,
        )

    held = [pieces[0]] + [None] * (QUAD - 1)
    for o in order:
        held[o] = moved(pieces[o], swap_quad(o))
    mine, rest = call(sum_kernel, [one, one], [where, *held], 1000, grant=2)
    other = moved(rest, swap_lane)
    pair, both = call(pair_kernel, [two, one], [where, mine, other], 1000, grant=2)
    shifts = [(dr, df) for dr in range(counts[0]) for df in range(counts[1]) if dr or df]
    shifts.sort(key=lambda shift_by: -sum(shift_by))
    came = []
    for dr, df in shifts:
        came.append(moved(both if dr else pair, shift(dr, df)))
    kernel = functools.partial(base_kernel, shifts, counts, reverse)
    sum_mine, sum_other = call(kernel, [one, one], [where, pair, *came], 1000, grant=2)
    other = moved(sum_other, swap_lane)
    kernel = functools.partial(back_sum_kernel, reverse)
    back = call(kernel, [two] * QUAD, [where, sum_mine, other, *held], 1000, grant=2)
    result = [back[0]] + [None] * (QUAD - 1)
    for o in order:
        result[o] = moved(back[o], swap_quad(o))
    return result


def body(queries, key_rows, value_rows, norm_gain, cotangent):
    grp, seq = lax.axis_index("grp"), lax.axis_index("seq")
    parts = [grp % LANES, seq % QUAD, grp // LANES, seq // QUAD]
    where = jnp.stack(parts).astype(jnp.int32)
    *pieces, inside, keys, values = totals(where, key_rows, value_rows)
    queries = near(queries)
    local = local_part(where, queries, keys, values)
    prior = carry(where, pieces, False)
    normed, grads, prior_half, *rest = middle(
        where, local, queries, cotangent, norm_gain[None, :], prior, inside
    )
    grad_pieces, later = rest[:QUAD], rest[QUAD]
    after = carry(where, grad_pieces, True)
    local_v, normed = turned_part(where, keys, queries, grads, normed)
    grad_q = query_part(where, grads, values, keys, prior_half)
    local_k, grad_q = turned_part(where, values, grads, queries, grad_q)
    grad_k, grad_v = final_part(where, local_k, local_v, keys, values, after, later)
    return normed, grad_q, grad_k, grad_v


def solution(mesh):
    rows = P(AXES, None)
    return jax.shard_map(
        body,
        mesh=mesh,
        in_specs=(rows, rows, rows, P(), rows),
        out_specs=(rows, rows, rows, rows),
        check_vma=False,
    )
```

```python
import functools

import jax
import jax.numpy as jnp
from jax import lax
from jax.experimental import pallas as pl
from jax.experimental.pallas import tpu as pltpu
from jax.sharding import PartitionSpec as P


H = 8
HD = 128
BLOCK = 512
EPSILON = 1e-06
AXES = ("grp", "seq")
LANES = 2
QUAD = 4
SHARE = H // (LANES * QUAD)
TILE = 256
CUT = 256
SLAB = 256
ORDER = (3, 1, 2, 0)
EARLY = (0, 3)
UNROLL = 4
PAIR = 2
UNROLL_FINAL = 4
DEPTH = 2
F32 = jnp.float32
BF16 = jnp.bfloat16


def mm(a, b, ca, cb):
    return lax.dot_general(a, b, (((ca,), (cb,)), ((), ())), preferred_element_type=F32)


def vmem(*shape, dtype=F32):
    return pltpu.VMEM(shape, dtype)


def near(value):
    return pltpu.with_memory_space_constraint(value, pltpu.VMEM)


def far(value):
    return pltpu.with_memory_space_constraint(value, pltpu.HBM)


def call(kernel, out_shape, args, flops, scratch=(), grant=8, far_in=(), far_out=(), aliases=None):
    any_space = pl.BlockSpec(memory_space=pltpu.HBM)
    near_space = pl.BlockSpec(memory_space=pltpu.VMEM)
    in_specs = [pl.BlockSpec(memory_space=pltpu.SMEM)]
    in_specs += [any_space if i in far_in else near_space for i in range(len(args) - 1)]
    out_specs = [any_space if i in far_out else near_space for i in range(len(out_shape))]
    args = [args[0]] + [far(a) if i in far_in else near(a) for i, a in enumerate(args[1:])]
    return pl.pallas_call(
        kernel,
        out_shape=out_shape,
        in_specs=in_specs,
        out_specs=out_specs,
        scratch_shapes=scratch,
        input_output_aliases=aliases or {},
        compiler_params=pltpu.CompilerParams(vmem_limit_bytes=grant << 20),
        cost_estimate=pl.CostEstimate(flops=flops, bytes_accessed=flops // 100, transcendentals=0),
    )(*args)


def head_cols(head):
    return pl.ds(pl.multiple_of(head * HD, HD), HD)


def over_heads(step, unroll):
    def several(i, _):
        for j in range(unroll):
            step(i * unroll + j)
        return 0

    lax.fori_loop(0, H // unroll, several, 0)


def heads_of(slot, where):
    for lane in range(LANES):
        for share in range(SHARE):
            unit = (where[0] ^ lane) * QUAD + (where[1] ^ slot)
            yield lane, share, unit * SHARE + share


def slot_block(slot, reverse, where, block, blocks, a_ref, b_ref, piece_ref, inside_ref):
    rows = pl.ds(block * BLOCK, BLOCK)
    for lane, share, head in heads_of(slot, where):
        cols = head_cols(head)
        state = mm(a_ref[rows, cols], b_ref[rows, cols], 0, 0)
        if block == (blocks - 1 if reverse else 0):
            inside_ref[block, lane, share] = jnp.zeros_like(state)
            piece_ref[lane, share] = state
        else:
            run = piece_ref[lane, share]
            inside_ref[block, lane, share] = run
            piece_ref[lane, share] = run + state


def slot_kernel(slots, reverse, where, a_ref, b_ref, *outs):
    blocks = a_ref.shape[0] // BLOCK
    for i, slot in enumerate(slots):
        for block in reversed(range(blocks)) if reverse else range(blocks):
            slot_block(slot, reverse, where, block, blocks, a_ref, b_ref, *outs[2 * i : 2 * i + 2])


def slot_shapes(blocks):
    return [vmem(LANES, SHARE, HD, HD), vmem(blocks, LANES, SHARE, HD, HD)]


def slot_totals(slots, reverse, where, a, b):
    tokens, features = a.shape
    outs = call(
        functools.partial(slot_kernel, slots, reverse),
        slot_shapes(tokens // BLOCK) * len(slots),
        [where, a, b],
        2 * tokens * features // QUAD * len(slots) * HD,
    )
    return {slot: outs[2 * i : 2 * i + 2] for i, slot in enumerate(slots)}


def load_kernel(slot, where, k_far, v_far, piece_ref, inside_ref, k_ref, v_ref, sems):
    blocks = k_ref.shape[0] // BLOCK
    copies = []
    for block in range(blocks):
        rows = pl.ds(block * BLOCK, BLOCK)
        for j, (source, target) in enumerate(((k_far, k_ref), (v_far, v_ref))):
            copy = pltpu.make_async_copy(source.at[rows, :], target.at[rows, :], sems.at[block, j])
            copies.append(copy)
    for copy in copies[: 2 * DEPTH]:
        copy.start()
    for block in range(blocks):
        for j in range(2):
            copies[2 * block + j].wait()
            if block + DEPTH < blocks:
                copies[2 * (block + DEPTH) + j].start()
        slot_block(slot, False, where, block, blocks, k_ref, v_ref, piece_ref, inside_ref)


def load_totals(slot, where, keys, values):
    tokens, features = keys.shape
    blocks = tokens // BLOCK
    return call(
        functools.partial(load_kernel, slot),
        slot_shapes(blocks) + [vmem(tokens, features, dtype=BF16)] * 2,
        [where, keys, values],
        2 * tokens * features * HD,
        scratch=[pltpu.SemaphoreType.DMA((blocks, 2))],
        far_in=(0, 1),
    )


def triangle(size, upper=False):
    row = lax.broadcasted_iota(jnp.int32, (size, size), 0)
    col = lax.broadcasted_iota(jnp.int32, (size, size), 1)
    return row <= col if upper else row >= col


def over_units(count, step):
    def several(i, _):
        for j in range(UNROLL):
            unit = i * UNROLL + j
            step(unit // H, unit % H)
        return 0

    lax.fori_loop(0, count // UNROLL, several, 0)


def block_part(block, first, count):
    return pl.ds(pl.multiple_of(block * BLOCK + first * CUT, CUT), count * CUT)


def attend(block, cols, a_ref, b_ref, c_ref, mask, turned):
    tiles = BLOCK // CUT
    sums = [None] * tiles
    for j in range(tiles):
        first, count = (0, j + 1) if turned else (j, tiles - j)
        rows, here = block_part(block, first, count), block_part(block, j, 1)
        scores = mm(a_ref[rows, cols], b_ref[here, cols], 1, 1)
        at = (j - first) * CUT
        parts = [jnp.where(mask, scores[at : at + CUT], 0.0)]
        if at:
            parts.insert(0, scores[:at])
        if at + CUT < count * CUT:
            parts.append(scores[at + CUT :])
        scores = jnp.concatenate([part.astype(BF16) for part in parts], axis=0)
        product = mm(scores, c_ref[here, cols], 1, 0)
        for i in range(count):
            value = product[i * CUT : (i + 1) * CUT]
            sums[first + i] = value if sums[first + i] is None else sums[first + i] + value
    return sums


def local_kernel(where, q_ref, k_ref, v_ref, out_ref):
    mask = triangle(CUT)

    def step(block, head):
        cols = head_cols(head)
        sums = attend(block, cols, q_ref, k_ref, v_ref, mask, False)
        for i, value in enumerate(sums):
            out_ref[block_part(block, i, 1), cols] = value

    over_units(q_ref.shape[0] // BLOCK * H, step)


def local_part(where, queries, keys, values):
    tokens, features = queries.shape
    return call(
        local_kernel,
        [vmem(tokens, features)],
        [where, queries, keys, values],
        4 * tokens * BLOCK * features,
    )[0]


def scores_kernel(where, k_ref, q_ref, out_ref):
    mask = triangle(CUT, True)

    def step(block, head):
        cols = head_cols(head)
        for j in range(BLOCK // CUT):
            rows, here = block_part(block, 0, j + 1), block_part(block, j, 1)
            scores = mm(k_ref[rows, cols], q_ref[here, cols], 1, 1)
            to = pl.ds(j * CUT, CUT)
            out_ref[block, head, to, to] = jnp.where(mask, scores[j * CUT :], 0.0).astype(BF16)
            if j:
                out_ref[block, head, pl.ds(0, j * CUT), to] = scores[: j * CUT].astype(BF16)

    over_units(k_ref.shape[0] // BLOCK * H, step)


def turned_scores(where, keys, queries):
    tokens, features = keys.shape
    return call(
        scores_kernel,
        [vmem(tokens // BLOCK, H, BLOCK, BLOCK, dtype=BF16)],
        [where, keys, queries],
        2 * tokens * BLOCK * features,
    )[0]


def value_kernel(where, scores_ref, g_ref, ready_ref, out_ref, far_ref, sem):
    copy = pltpu.make_async_copy(ready_ref, far_ref, sem)
    copy.start()

    def step(block, head):
        cols = head_cols(head)
        tiles = BLOCK // CUT
        sums = [None] * tiles
        for j in range(tiles):
            rows = pl.ds(0, (j + 1) * CUT)
            scores = scores_ref[block, head, rows, pl.ds(j * CUT, CUT)]
            product = mm(scores, g_ref[block_part(block, j, 1), cols], 1, 0)
            for i in range(j + 1):
                value = product[i * CUT : (i + 1) * CUT]
                sums[i] = value if sums[i] is None else sums[i] + value
        for i, value in enumerate(sums):
            out_ref[block_part(block, i, 1), cols] = value

    over_units(g_ref.shape[0] // BLOCK * H, step)
    copy.wait()


def value_part(where, scores, grads, ready):
    tokens, features = grads.shape
    return call(
        value_kernel,
        [vmem(tokens, features), jax.ShapeDtypeStruct(ready.shape, ready.dtype)],
        [where, scores, grads, ready],
        2 * tokens * BLOCK * features,
        scratch=[pltpu.SemaphoreType.DMA(())],
        far_out=(1,),
    )


def attended_kernel(slot, first, where, carried_ref, inside_ref, local_ref, q_ref, dy_ref, gain_ref, *refs):
    if first:
        att_ref, square_ref, cross_ref, prior_ref = refs
    else:
        old_square, old_cross, att_ref, square_ref, cross_ref, prior_ref = refs
    blocks = q_ref.shape[0] // BLOCK
    for block in range(blocks):
        rows = pl.ds(block * BLOCK, BLOCK)
        square = None if first else old_square[rows, :]
        cross = None if first else old_cross[rows, :]
        for lane, share, head in heads_of(slot, where):
            cols = head_cols(head)
            prior = (carried_ref[lane, share] + inside_ref[block, lane, share]).astype(BF16)
            prior_ref[block, lane, share] = prior
            att = local_ref[rows, cols] + mm(q_ref[rows, cols], prior, 1, 0)
            att_ref[rows, cols] = att
            term = dy_ref[rows, cols].astype(F32) * gain_ref[:, cols] * att
            square = att * att if square is None else square + att * att
            cross = term if cross is None else cross + term
        square_ref[rows, :] = square
        cross_ref[rows, :] = cross


def attended_slot(slot, where, carried, inside, local, queries, cotangent, gain, sums):
    tokens, features = queries.shape
    blocks = tokens // BLOCK
    first = not sums
    return call(
        functools.partial(attended_kernel, slot, first),
        [vmem(tokens, features), vmem(tokens, HD), vmem(tokens, HD)]
        + [vmem(blocks, LANES, SHARE, HD, HD, dtype=BF16)],
        [where, carried, inside, local, queries, cotangent, gain, *sums],
        2 * tokens * features // QUAD * HD,
        aliases={3: 0},
    )


def norm_kernel(slots, where, *refs):
    count = len(slots)
    carried, inside = refs[:count], refs[count : 2 * count]
    local_ref, q_ref, dy_ref, gain_ref, old_square, old_cross = refs[2 * count : 2 * count + 6]
    outs = refs[2 * count + 6 :]
    att_ref, out_ref, grad_ref = outs[:3]
    priors, (piece_ref, later_ref, square_ref, cross_ref) = outs[3 : 3 + count], outs[3 + count :]
    blocks = q_ref.shape[0] // BLOCK
    features = H * HD
    for block in reversed(range(blocks)):
        rows = pl.ds(block * BLOCK, BLOCK)
        square, cross = old_square[rows, :], old_cross[rows, :]
        for i, slot in enumerate(slots):
            for lane, share, head in heads_of(slot, where):
                cols = head_cols(head)
                prior = (carried[i][lane, share] + inside[i][block, lane, share]).astype(BF16)
                priors[i][block, lane, share] = prior
                att = local_ref[rows, cols] + mm(q_ref[rows, cols], prior, 1, 0)
                att_ref[rows, cols] = att
                square += att * att
                cross += dy_ref[rows, cols].astype(F32) * gain_ref[:, cols] * att
        square_ref[...], cross_ref[...] = square, cross

        def step(i, _):
            here = pl.ds(pl.multiple_of(i * SLAB, SLAB), SLAB)
            rows = pl.ds(pl.multiple_of(block * BLOCK + i * SLAB, SLAB), SLAB)
            square = jnp.sum(square_ref[here, :], axis=1, keepdims=True) / features
            inverse = lax.rsqrt(square + EPSILON)
            mean = inverse * (jnp.sum(cross_ref[here, :], axis=1, keepdims=True) / features)
            for head in range(H):
                cols = pl.ds(head * HD, HD)
                unit = att_ref[rows, cols] * inverse
                gain = gain_ref[:, cols]
                out_ref[rows, cols] = (unit * gain).astype(BF16)
                scaled = dy_ref[rows, cols].astype(F32) * gain
                grad_ref[rows, cols] = (inverse * (scaled - unit * mean)).astype(BF16)
            return 0

        lax.fori_loop(0, BLOCK // SLAB, step, 0)
        slot_block(ORDER[0], True, where, block, blocks, q_ref, grad_ref, piece_ref, later_ref)


def norm(slots, where, carried, inside, attended, queries, cotangent, gain, sums):
    tokens, features = attended.shape
    blocks = tokens // BLOCK
    half = vmem(tokens, features, dtype=BF16)
    prior = vmem(blocks, LANES, SHARE, HD, HD, dtype=BF16)
    carried, inside = [carried[o] for o in slots], [inside[o] for o in slots]
    _, normed, grads, *outs = call(
        functools.partial(norm_kernel, slots),
        [vmem(tokens, features), half, half] + [prior] * len(slots) + slot_shapes(blocks),
        [where, *carried, *inside, attended, queries, cotangent, gain, *sums],
        20 * tokens * features,
        scratch=[vmem(BLOCK, HD)] * 2,
        aliases={1 + 2 * len(slots): 0},
    )
    return normed, grads, outs[: len(slots)], outs[len(slots) :]


def query_kernel(where, g_ref, v_ref, k_ref, *refs):
    priors, (out_ref, prior_ref) = refs[:QUAD], refs[QUAD:]
    mask = triangle(CUT)
    prior_ref[...] = jnp.zeros_like(prior_ref)
    for slot in range(QUAD):
        for lane, share, head in heads_of(slot, where):
            cols = head_cols(head % PAIR)
            for block in range(prior_ref.shape[0]):
                prior_ref[block, head // PAIR, cols, cols] = priors[slot][block, lane, share]

    def step(block, pair):
        wide = pl.ds(pl.multiple_of(pair * PAIR * HD, PAIR * HD), PAIR * HD)
        rows = block_part(block, 0, BLOCK // CUT)
        far_part = mm(g_ref[rows, wide], prior_ref[block, pair], 1, 1)
        for j in range(PAIR):
            cols = head_cols(pair * PAIR + j)
            sums = attend(block, cols, g_ref, v_ref, k_ref, mask, False)
            for i, value in enumerate(sums):
                value += far_part[i * CUT : (i + 1) * CUT, j * HD : (j + 1) * HD]
                out_ref[block_part(block, i, 1), cols] = value.astype(BF16)

    def several(i, _):
        for j in range(UNROLL // PAIR):
            unit = i * (UNROLL // PAIR) + j
            step(unit // (H // PAIR), unit % (H // PAIR))
        return 0

    lax.fori_loop(0, g_ref.shape[0] // BLOCK * H // UNROLL, several, 0)


def query_part(where, grads, values, keys, priors):
    tokens, features = grads.shape
    return call(
        query_kernel,
        [vmem(tokens, features, dtype=BF16)],
        [where, grads, values, keys, *priors],
        4 * tokens * BLOCK * features,
        scratch=[vmem(tokens // BLOCK, H // PAIR, PAIR * HD, PAIR * HD, dtype=BF16)],
    )[0]


def turned_kernel(where, a_ref, b_ref, c_ref, ready_ref, out_ref, far_ref, sem):
    copy = pltpu.make_async_copy(ready_ref, far_ref, sem)
    copy.start()
    mask = triangle(CUT, True)

    def step(block, head):
        cols = head_cols(head)
        sums = attend(block, cols, a_ref, b_ref, c_ref, mask, True)
        for i, value in enumerate(sums):
            out_ref[block_part(block, i, 1), cols] = value

    over_units(a_ref.shape[0] // BLOCK * H, step)
    copy.wait()


def turned_part(where, a, b, c, ready):
    tokens, features = a.shape
    return call(
        turned_kernel,
        [vmem(tokens, features), jax.ShapeDtypeStruct(ready.shape, ready.dtype)],
        [where, a, b, c, ready],
        4 * tokens * BLOCK * features,
        scratch=[pltpu.SemaphoreType.DMA(())],
        far_out=(1,),
    )


def final_kernel(where, lk_ref, lv_ref, k_ref, v_ref, *refs):
    carried, later = refs[:QUAD], refs[QUAD : 2 * QUAD]
    gk_far, gv_far, gk_ref, gv_ref, state_ref, sems = refs[2 * QUAD :]
    for slot in range(QUAD):
        for lane, share, head in heads_of(slot, where):
            for b in range(k_ref.shape[0] // BLOCK):
                state = carried[slot][lane, share] + later[slot][b, lane, share]
                state_ref[b, head] = state.astype(BF16)

    copies = []
    for i in range(k_ref.shape[0] // TILE):
        rows = pl.ds(i * TILE, TILE)
        block = i // (BLOCK // TILE)

        def one(head):
            cols = head_cols(head)
            state = state_ref[block, head]
            gk_ref[rows, cols] = (lk_ref[rows, cols] + mm(v_ref[rows, cols], state, 1, 1)).astype(BF16)
            gv_ref[rows, cols] = (lv_ref[rows, cols] + mm(k_ref[rows, cols], state, 1, 0)).astype(BF16)

        over_heads(one, UNROLL_FINAL)
        for j, (source, target) in enumerate(((gk_ref, gk_far), (gv_ref, gv_far))):
            copy = pltpu.make_async_copy(source.at[rows, :], target.at[rows, :], sems.at[i, j])
            copy.start()
            copies.append(copy)
    for copy in copies:
        copy.wait()


def final_part(where, local_k, local_v, keys, values, carried, later):
    tokens, features = keys.shape
    blocks = tokens // BLOCK
    return call(
        final_kernel,
        [jax.ShapeDtypeStruct((tokens, features), BF16)] * 2,
        [where, local_k, local_v, keys, values, *carried, *later],
        4 * tokens * features * HD,
        scratch=[
            vmem(tokens, features, dtype=BF16),
            vmem(tokens, features, dtype=BF16),
            vmem(blocks, H, HD, HD, dtype=BF16),
            pltpu.SemaphoreType.DMA((tokens // TILE, 2)),
        ],
        far_out=(0, 1),
        grant=12,
    )


def moved(value, move):
    groups, shards = lax.axis_size("grp"), lax.axis_size("seq")
    pairs = []
    for g in range(groups):
        for s in range(shards):
            to_g, to_s = move(g, s)
            pairs.append((g * shards + s, to_g * shards + to_s))
    return lax.ppermute(value, AXES, pairs)


def sum_kernel(where, *refs):
    held, (mine_ref, rest_ref) = refs[:QUAD], refs[QUAD:]
    for lane, out in enumerate((mine_ref, rest_ref)):
        out[...] = (held[0][lane] + held[1][lane]) + (held[2][lane] + held[3][lane])


def both_kernel(where, mine_ref, other_ref, both_ref):
    both_ref[...] = mine_ref[...] + other_ref[...]


def before(a, b, reverse):
    return a > b if reverse else a < b


def base_kernel(near_shifts, far_shifts, counts, reverse, where, mine_ref, other_ref, *refs):
    refs = list(refs)
    lane, row, far_row = where[0], where[2], where[3]
    takes = lane == (0 if reverse else 1)
    sum_mine = jnp.where(takes, other_ref[...], 0.0)
    sum_other = jnp.where(takes, 0.0, mine_ref[...])
    near_mine = [refs.pop(0) for _ in near_shifts]
    near_other = [refs.pop(0) for _ in near_shifts]
    for df, mine, other in zip(near_shifts, near_mine, near_other):
        near_by = before(lax.rem(far_row - df + counts[1], counts[1]), far_row, reverse)
        mine, other = mine[...], other[...]
        sum_mine += jnp.where(near_by, mine, 0.0) + jnp.where(takes, other, 0.0)
        sum_other += jnp.where(near_by, other, 0.0) + jnp.where(takes, 0.0, mine)
    for dr, _ in far_shifts:
        source = lax.rem(row - dr + counts[0], counts[0])
        add = jnp.where(before(source, row, reverse), refs.pop(0)[...], 0.0)
        sum_mine, sum_other = sum_mine + add, sum_other + add
    refs[0][...], refs[1][...] = sum_mine, sum_other


def back_sum_kernel(reverse, where, mine_ref, other_ref, *refs):
    held, back = refs[:QUAD], refs[QUAD:]
    quad = where[1]
    for lane, base in enumerate((mine_ref, other_ref)):
        for o in range(QUAD):
            value = base[...]
            for i in range(QUAD):
                if i != o:
                    near_by = before(quad ^ i, quad ^ o, reverse)
                    value += jnp.where(near_by, held[i][lane], 0.0)
            back[o][lane] = value


def far_shifts_of(counts):
    shifts = [(dr, df) for dr in range(1, counts[0]) for df in range(counts[1])]
    return sorted(shifts, key=lambda shift: -sum(shift))


def carry(where, first, rest, reverse):
    counts = lax.axis_size("grp") // LANES, lax.axis_size("seq") // QUAD
    one, two = vmem(SHARE, HD, HD), vmem(LANES, SHARE, HD, HD)

    def swap_quad(o):
        return lambda g, s: (g, s ^ o)

    def swap_lane(g, s):
        return g ^ 1, s

    def shift(dr, df):
        return lambda g, s: (
            (g // LANES + dr) % counts[0] * LANES + g % LANES,
            (s // QUAD + df) % counts[1] * QUAD + s % QUAD,
        )

    held, inside = [None] * QUAD, [None] * QUAD
    held[ORDER[0]], inside[ORDER[0]] = first
    held[ORDER[0]] = moved(held[ORDER[0]], swap_quad(ORDER[0]))
    rest = slot_totals(ORDER[1:], reverse, where, *rest)
    for o in ORDER[1:]:
        held[o], inside[o] = rest[o]
        if o:
            held[o] = moved(held[o], swap_quad(o))
    mine, rest = call(sum_kernel, [one, one], [where, *held], 1000, grant=2)
    near_shifts, far_shifts = range(1, counts[1]), far_shifts_of(counts)
    came_mine, came_other, came_both = [], [], []
    for df in near_shifts:
        came_mine.append(moved(mine, shift(0, df)))
    other = moved(rest, swap_lane)
    for df in near_shifts:
        came_other.append(moved(other, shift(0, df)))
    both = call(both_kernel, [one], [where, mine, other], 1000, grant=2)[0]
    for dr, df in far_shifts:
        came_both.append(moved(both, shift(dr, df)))
    kernel = functools.partial(base_kernel, near_shifts, far_shifts, counts, reverse)
    args = [where, mine, other, *came_mine, *came_other, *came_both]
    sum_mine, sum_other = call(kernel, [one, one], args, 1000, grant=2)
    other = moved(sum_other, swap_lane)
    kernel = functools.partial(back_sum_kernel, reverse)
    back = call(kernel, [two] * QUAD, [where, sum_mine, other, *held], 1000, grant=2)
    result = [back[0]] + [None] * (QUAD - 1)
    for o in ORDER[:-1]:
        result[o] = moved(back[o], swap_quad(o))
    return result, inside


def body(queries, key_rows, value_rows, norm_gain, cotangent):
    grp, seq = lax.axis_index("grp"), lax.axis_index("seq")
    parts = [grp % LANES, seq % QUAD, grp // LANES, seq // QUAD]
    where = jnp.stack(parts).astype(jnp.int32)
    gain = norm_gain[None, :]
    *first, keys, values = load_totals(ORDER[0], where, key_rows, value_rows)
    queries, cotangent = near(queries), near(cotangent)
    carried, inside = carry(where, first, (keys, values), False)
    attended = local_part(where, queries, keys, values)
    scores = turned_scores(where, keys, queries)
    priors, sums = [None] * QUAD, []
    for o in EARLY:
        attended, *sums, priors[o] = attended_slot(
            o, where, carried[o], inside[o], attended, queries, cotangent, gain, sums
        )
    late = [o for o in ORDER if o not in EARLY]
    normed, grads, late_priors, first = norm(
        late, where, carried, inside, attended, queries, cotangent, gain, sums
    )
    for o, prior in zip(late, late_priors):
        priors[o] = prior
    carried, later = carry(where, first, (queries, grads), True)
    local_v, normed = value_part(where, scores, grads, normed)
    grad_q = query_part(where, grads, values, keys, priors)
    local_k, grad_q = turned_part(where, values, grads, queries, grad_q)
    grad_k, grad_v = final_part(where, local_k, local_v, keys, values, carried, later)
    return normed, grad_q, grad_k, grad_v


def solution(mesh):
    rows = P(AXES, None)
    return jax.shard_map(
        body,
        mesh=mesh,
        in_specs=(rows, rows, rows, P(), rows),
        out_specs=(rows, rows, rows, rows),
        check_vma=False,
    )
```

```python
import functools

import jax
import jax.numpy as jnp
from jax import lax
from jax.experimental import pallas as pl
from jax.experimental.pallas import tpu as pltpu
from jax.sharding import PartitionSpec as P


H = 8
HD = 128
BLOCK = 512
EPSILON = 1e-06
AXES = ("grp", "seq")
LANES = 2
QUAD = 4
SHARE = H // (LANES * QUAD)
TILE = 256
CUT = 256
SLAB = 256
ORDER = (3, 1, 2, 0)
EARLY = (0, 3)
UNROLL = 4
PAIR = 2
UNROLL_FINAL = 4
DEPTH = 2
F32 = jnp.float32
BF16 = jnp.bfloat16


def mm(a, b, ca, cb):
    return lax.dot_general(a, b, (((ca,), (cb,)), ((), ())), preferred_element_type=F32)


def vmem(*shape, dtype=F32):
    return pltpu.VMEM(shape, dtype)


def near(value):
    return pltpu.with_memory_space_constraint(value, pltpu.VMEM)


def far(value):
    return pltpu.with_memory_space_constraint(value, pltpu.HBM)


def place():
    grp, seq = lax.axis_index("grp"), lax.axis_index("seq")
    return lax.rem(grp, LANES), lax.rem(seq, QUAD), lax.div(grp, LANES), lax.div(seq, QUAD)


def call(kernel, out_shape, args, flops, scratch=(), grant=8, far_in=(), far_out=(), aliases=None):
    any_space = pl.BlockSpec(memory_space=pltpu.HBM)
    near_space = pl.BlockSpec(memory_space=pltpu.VMEM)
    return pl.pallas_call(
        lambda *refs: kernel(place(), *refs),
        out_shape=out_shape,
        in_specs=[any_space if i in far_in else near_space for i in range(len(args))],
        out_specs=[any_space if i in far_out else near_space for i in range(len(out_shape))],
        scratch_shapes=scratch,
        input_output_aliases=aliases or {},
        compiler_params=pltpu.CompilerParams(vmem_limit_bytes=grant << 20),
        cost_estimate=pl.CostEstimate(flops=flops, bytes_accessed=flops // 100, transcendentals=0),
    )(*[far(a) if i in far_in else near(a) for i, a in enumerate(args)])


def head_cols(head):
    return pl.ds(pl.multiple_of(head * HD, HD), HD)


def over_heads(step, unroll):
    def several(i, _):
        for j in range(unroll):
            step(i * unroll + j)
        return 0

    lax.fori_loop(0, H // unroll, several, 0)


def heads_of(slot, where):
    for lane in range(LANES):
        for share in range(SHARE):
            unit = (where[0] ^ lane) * QUAD + (where[1] ^ slot)
            yield lane, share, unit * SHARE + share


def slot_block(slot, reverse, where, block, blocks, a_ref, b_ref, piece_ref, inside_ref):
    rows = pl.ds(block * BLOCK, BLOCK)
    for lane, share, head in heads_of(slot, where):
        cols = head_cols(head)
        state = mm(a_ref[rows, cols], b_ref[rows, cols], 0, 0)
        if block == (blocks - 1 if reverse else 0):
            inside_ref[block, lane, share] = jnp.zeros_like(state)
            piece_ref[lane, share] = state
        else:
            run = piece_ref[lane, share]
            inside_ref[block, lane, share] = run
            piece_ref[lane, share] = run + state


def slot_kernel(slots, reverse, where, a_ref, b_ref, *outs):
    blocks = a_ref.shape[0] // BLOCK
    for i, slot in enumerate(slots):
        for block in reversed(range(blocks)) if reverse else range(blocks):
            slot_block(slot, reverse, where, block, blocks, a_ref, b_ref, *outs[2 * i : 2 * i + 2])


def slot_shapes(blocks):
    return [vmem(LANES, SHARE, HD, HD), vmem(blocks, LANES, SHARE, HD, HD)]


def slot_totals(slots, reverse, a, b):
    tokens, features = a.shape
    outs = call(
        functools.partial(slot_kernel, slots, reverse),
        slot_shapes(tokens // BLOCK) * len(slots),
        [a, b],
        2 * tokens * features // QUAD * len(slots) * HD,
    )
    return {slot: outs[2 * i : 2 * i + 2] for i, slot in enumerate(slots)}


def load_kernel(slot, where, k_far, v_far, piece_ref, inside_ref, k_ref, v_ref, sems):
    blocks = k_ref.shape[0] // BLOCK
    copies = []
    for block in range(blocks):
        rows = pl.ds(block * BLOCK, BLOCK)
        for j, (source, target) in enumerate(((k_far, k_ref), (v_far, v_ref))):
            copy = pltpu.make_async_copy(source.at[rows, :], target.at[rows, :], sems.at[block, j])
            copies.append(copy)
    for copy in copies[: 2 * DEPTH]:
        copy.start()
    for block in range(blocks):
        for j in range(2):
            copies[2 * block + j].wait()
            if block + DEPTH < blocks:
                copies[2 * (block + DEPTH) + j].start()
        slot_block(slot, False, where, block, blocks, k_ref, v_ref, piece_ref, inside_ref)


def load_totals(slot, keys, values):
    tokens, features = keys.shape
    blocks = tokens // BLOCK
    return call(
        functools.partial(load_kernel, slot),
        slot_shapes(blocks) + [vmem(tokens, features, dtype=BF16)] * 2,
        [keys, values],
        2 * tokens * features * HD,
        scratch=[pltpu.SemaphoreType.DMA((blocks, 2))],
        far_in=(0, 1),
    )


def triangle(size, upper=False):
    row = lax.broadcasted_iota(jnp.int32, (size, size), 0)
    col = lax.broadcasted_iota(jnp.int32, (size, size), 1)
    return row <= col if upper else row >= col


def over_units(count, step):
    def several(i, _):
        for j in range(UNROLL):
            unit = i * UNROLL + j
            step(unit // H, unit % H)
        return 0

    lax.fori_loop(0, count // UNROLL, several, 0)


def block_part(block, first, count):
    return pl.ds(pl.multiple_of(block * BLOCK + first * CUT, CUT), count * CUT)


def attend(block, cols, a_ref, b_ref, c_ref, mask, turned):
    tiles = BLOCK // CUT
    sums = [None] * tiles
    for j in range(tiles):
        first, count = (0, j + 1) if turned else (j, tiles - j)
        rows, here = block_part(block, first, count), block_part(block, j, 1)
        scores = mm(a_ref[rows, cols], b_ref[here, cols], 1, 1)
        at = (j - first) * CUT
        parts = [jnp.where(mask, scores[at : at + CUT], 0.0)]
        if at:
            parts.insert(0, scores[:at])
        if at + CUT < count * CUT:
            parts.append(scores[at + CUT :])
        scores = jnp.concatenate([part.astype(BF16) for part in parts], axis=0)
        product = mm(scores, c_ref[here, cols], 1, 0)
        for i in range(count):
            value = product[i * CUT : (i + 1) * CUT]
            sums[first + i] = value if sums[first + i] is None else sums[first + i] + value
    return sums


def local_kernel(where, q_ref, k_ref, v_ref, out_ref):
    mask = triangle(CUT)

    def step(block, head):
        cols = head_cols(head)
        sums = attend(block, cols, q_ref, k_ref, v_ref, mask, False)
        for i, value in enumerate(sums):
            out_ref[block_part(block, i, 1), cols] = value

    over_units(q_ref.shape[0] // BLOCK * H, step)


def local_part(queries, keys, values):
    tokens, features = queries.shape
    return call(
        local_kernel,
        [vmem(tokens, features)],
        [queries, keys, values],
        4 * tokens * BLOCK * features,
    )[0]


def scores_kernel(where, k_ref, q_ref, out_ref):
    mask = triangle(CUT, True)

    def step(block, head):
        cols = head_cols(head)
        for j in range(BLOCK // CUT):
            rows, here = block_part(block, 0, j + 1), block_part(block, j, 1)
            scores = mm(k_ref[rows, cols], q_ref[here, cols], 1, 1)
            to = pl.ds(j * CUT, CUT)
            out_ref[block, head, to, to] = jnp.where(mask, scores[j * CUT :], 0.0).astype(BF16)
            if j:
                out_ref[block, head, pl.ds(0, j * CUT), to] = scores[: j * CUT].astype(BF16)

    over_units(k_ref.shape[0] // BLOCK * H, step)


def turned_scores(keys, queries):
    tokens, features = keys.shape
    return call(
        scores_kernel,
        [vmem(tokens // BLOCK, H, BLOCK, BLOCK, dtype=BF16)],
        [keys, queries],
        2 * tokens * BLOCK * features,
    )[0]


def value_kernel(where, scores_ref, g_ref, ready_ref, out_ref, far_ref, sem):
    copy = pltpu.make_async_copy(ready_ref, far_ref, sem)
    copy.start()

    def step(block, head):
        cols = head_cols(head)
        tiles = BLOCK // CUT
        sums = [None] * tiles
        for j in range(tiles):
            rows = pl.ds(0, (j + 1) * CUT)
            scores = scores_ref[block, head, rows, pl.ds(j * CUT, CUT)]
            product = mm(scores, g_ref[block_part(block, j, 1), cols], 1, 0)
            for i in range(j + 1):
                value = product[i * CUT : (i + 1) * CUT]
                sums[i] = value if sums[i] is None else sums[i] + value
        for i, value in enumerate(sums):
            out_ref[block_part(block, i, 1), cols] = value

    over_units(g_ref.shape[0] // BLOCK * H, step)
    copy.wait()


def value_part(scores, grads, ready):
    tokens, features = grads.shape
    return call(
        value_kernel,
        [vmem(tokens, features), jax.ShapeDtypeStruct(ready.shape, ready.dtype)],
        [scores, grads, ready],
        2 * tokens * BLOCK * features,
        scratch=[pltpu.SemaphoreType.DMA(())],
        far_out=(1,),
    )


def attended_kernel(slot, first, where, carried_ref, inside_ref, local_ref, q_ref, dy_ref, gain_ref, *refs):
    if first:
        att_ref, square_ref, cross_ref, prior_ref = refs
    else:
        old_square, old_cross, att_ref, square_ref, cross_ref, prior_ref = refs
    blocks = q_ref.shape[0] // BLOCK
    for block in range(blocks):
        rows = pl.ds(block * BLOCK, BLOCK)
        square = None if first else old_square[rows, :]
        cross = None if first else old_cross[rows, :]
        for lane, share, head in heads_of(slot, where):
            cols = head_cols(head)
            prior = (carried_ref[lane, share] + inside_ref[block, lane, share]).astype(BF16)
            prior_ref[block, lane, share] = prior
            att = local_ref[rows, cols] + mm(q_ref[rows, cols], prior, 1, 0)
            att_ref[rows, cols] = att
            term = dy_ref[rows, cols].astype(F32) * gain_ref[:, cols] * att
            square = att * att if square is None else square + att * att
            cross = term if cross is None else cross + term
        square_ref[rows, :] = square
        cross_ref[rows, :] = cross


def attended_slot(slot, carried, inside, local, queries, cotangent, gain, sums):
    tokens, features = queries.shape
    blocks = tokens // BLOCK
    first = not sums
    return call(
        functools.partial(attended_kernel, slot, first),
        [vmem(tokens, features), vmem(tokens, HD), vmem(tokens, HD)]
        + [vmem(blocks, LANES, SHARE, HD, HD, dtype=BF16)],
        [carried, inside, local, queries, cotangent, gain, *sums],
        2 * tokens * features // QUAD * HD,
        aliases={2: 0},
    )


def norm_kernel(slots, where, *refs):
    count = len(slots)
    carried, inside = refs[:count], refs[count : 2 * count]
    local_ref, q_ref, dy_ref, gain_ref, old_square, old_cross = refs[2 * count : 2 * count + 6]
    outs = refs[2 * count + 6 :]
    att_ref, out_ref, grad_ref = outs[:3]
    priors, (piece_ref, later_ref, square_ref, cross_ref) = outs[3 : 3 + count], outs[3 + count :]
    blocks = q_ref.shape[0] // BLOCK
    features = H * HD
    for block in reversed(range(blocks)):
        rows = pl.ds(block * BLOCK, BLOCK)
        square, cross = old_square[rows, :], old_cross[rows, :]
        for i, slot in enumerate(slots):
            for lane, share, head in heads_of(slot, where):
                cols = head_cols(head)
                prior = (carried[i][lane, share] + inside[i][block, lane, share]).astype(BF16)
                priors[i][block, lane, share] = prior
                att = local_ref[rows, cols] + mm(q_ref[rows, cols], prior, 1, 0)
                att_ref[rows, cols] = att
                square += att * att
                cross += dy_ref[rows, cols].astype(F32) * gain_ref[:, cols] * att
        square_ref[...], cross_ref[...] = square, cross

        def step(i, _):
            here = pl.ds(pl.multiple_of(i * SLAB, SLAB), SLAB)
            rows = pl.ds(pl.multiple_of(block * BLOCK + i * SLAB, SLAB), SLAB)
            square = jnp.sum(square_ref[here, :], axis=1, keepdims=True) / features
            inverse = lax.rsqrt(square + EPSILON)
            mean = inverse * (jnp.sum(cross_ref[here, :], axis=1, keepdims=True) / features)
            for head in range(H):
                cols = pl.ds(head * HD, HD)
                unit = att_ref[rows, cols] * inverse
                gain = gain_ref[:, cols]
                out_ref[rows, cols] = (unit * gain).astype(BF16)
                scaled = dy_ref[rows, cols].astype(F32) * gain
                grad_ref[rows, cols] = (inverse * (scaled - unit * mean)).astype(BF16)
            return 0

        lax.fori_loop(0, BLOCK // SLAB, step, 0)
        slot_block(ORDER[0], True, where, block, blocks, q_ref, grad_ref, piece_ref, later_ref)


def norm(slots, carried, inside, attended, queries, cotangent, gain, sums):
    tokens, features = attended.shape
    blocks = tokens // BLOCK
    half = vmem(tokens, features, dtype=BF16)
    prior = vmem(blocks, LANES, SHARE, HD, HD, dtype=BF16)
    carried, inside = [carried[o] for o in slots], [inside[o] for o in slots]
    _, normed, grads, *outs = call(
        functools.partial(norm_kernel, slots),
        [vmem(tokens, features), half, half] + [prior] * len(slots) + slot_shapes(blocks),
        [*carried, *inside, attended, queries, cotangent, gain, *sums],
        20 * tokens * features,
        scratch=[vmem(BLOCK, HD)] * 2,
        aliases={2 * len(slots): 0},
    )
    return normed, grads, outs[: len(slots)], outs[len(slots) :]


def query_kernel(where, g_ref, v_ref, k_ref, *refs):
    priors, (out_ref, prior_ref) = refs[:QUAD], refs[QUAD:]
    mask = triangle(CUT)
    prior_ref[...] = jnp.zeros_like(prior_ref)
    for slot in range(QUAD):
        for lane, share, head in heads_of(slot, where):
            cols = head_cols(head % PAIR)
            for block in range(prior_ref.shape[0]):
                prior_ref[block, head // PAIR, cols, cols] = priors[slot][block, lane, share]

    def step(block, pair):
        wide = pl.ds(pl.multiple_of(pair * PAIR * HD, PAIR * HD), PAIR * HD)
        rows = block_part(block, 0, BLOCK // CUT)
        far_part = mm(g_ref[rows, wide], prior_ref[block, pair], 1, 1)
        for j in range(PAIR):
            cols = head_cols(pair * PAIR + j)
            sums = attend(block, cols, g_ref, v_ref, k_ref, mask, False)
            for i, value in enumerate(sums):
                value += far_part[i * CUT : (i + 1) * CUT, j * HD : (j + 1) * HD]
                out_ref[block_part(block, i, 1), cols] = value.astype(BF16)

    def several(i, _):
        for j in range(UNROLL // PAIR):
            unit = i * (UNROLL // PAIR) + j
            step(unit // (H // PAIR), unit % (H // PAIR))
        return 0

    lax.fori_loop(0, g_ref.shape[0] // BLOCK * H // UNROLL, several, 0)


def query_part(grads, values, keys, priors):
    tokens, features = grads.shape
    return call(
        query_kernel,
        [vmem(tokens, features, dtype=BF16)],
        [grads, values, keys, *priors],
        4 * tokens * BLOCK * features,
        scratch=[vmem(tokens // BLOCK, H // PAIR, PAIR * HD, PAIR * HD, dtype=BF16)],
    )[0]


def turned_kernel(where, a_ref, b_ref, c_ref, ready_ref, out_ref, far_ref, sem):
    copy = pltpu.make_async_copy(ready_ref, far_ref, sem)
    copy.start()
    mask = triangle(CUT, True)

    def step(block, head):
        cols = head_cols(head)
        sums = attend(block, cols, a_ref, b_ref, c_ref, mask, True)
        for i, value in enumerate(sums):
            out_ref[block_part(block, i, 1), cols] = value

    over_units(a_ref.shape[0] // BLOCK * H, step)
    copy.wait()


def turned_part(a, b, c, ready):
    tokens, features = a.shape
    return call(
        turned_kernel,
        [vmem(tokens, features), jax.ShapeDtypeStruct(ready.shape, ready.dtype)],
        [a, b, c, ready],
        4 * tokens * BLOCK * features,
        scratch=[pltpu.SemaphoreType.DMA(())],
        far_out=(1,),
    )


def final_kernel(where, lk_ref, lv_ref, k_ref, v_ref, *refs):
    carried, later = refs[:QUAD], refs[QUAD : 2 * QUAD]
    gk_far, gv_far, gk_ref, gv_ref, state_ref, sems = refs[2 * QUAD :]
    for slot in range(QUAD):
        for lane, share, head in heads_of(slot, where):
            for b in range(k_ref.shape[0] // BLOCK):
                state = carried[slot][lane, share] + later[slot][b, lane, share]
                state_ref[b, head] = state.astype(BF16)

    copies = []
    for i in range(k_ref.shape[0] // TILE):
        rows = pl.ds(i * TILE, TILE)
        block = i // (BLOCK // TILE)

        def one(head):
            cols = head_cols(head)
            state = state_ref[block, head]
            gk_ref[rows, cols] = (lk_ref[rows, cols] + mm(v_ref[rows, cols], state, 1, 1)).astype(BF16)
            gv_ref[rows, cols] = (lv_ref[rows, cols] + mm(k_ref[rows, cols], state, 1, 0)).astype(BF16)

        over_heads(one, UNROLL_FINAL)
        for j, (source, target) in enumerate(((gk_ref, gk_far), (gv_ref, gv_far))):
            copy = pltpu.make_async_copy(source.at[rows, :], target.at[rows, :], sems.at[i, j])
            copy.start()
            copies.append(copy)
    for copy in copies:
        copy.wait()


def final_part(local_k, local_v, keys, values, carried, later):
    tokens, features = keys.shape
    blocks = tokens // BLOCK
    return call(
        final_kernel,
        [jax.ShapeDtypeStruct((tokens, features), BF16)] * 2,
        [local_k, local_v, keys, values, *carried, *later],
        4 * tokens * features * HD,
        scratch=[
            vmem(tokens, features, dtype=BF16),
            vmem(tokens, features, dtype=BF16),
            vmem(blocks, H, HD, HD, dtype=BF16),
            pltpu.SemaphoreType.DMA((tokens // TILE, 2)),
        ],
        far_out=(0, 1),
        grant=12,
    )


def moved(value, move):
    groups, shards = lax.axis_size("grp"), lax.axis_size("seq")
    pairs = []
    for g in range(groups):
        for s in range(shards):
            to_g, to_s = move(g, s)
            pairs.append((g * shards + s, to_g * shards + to_s))
    return lax.ppermute(value, AXES, pairs)


def sum_kernel(where, *refs):
    held, (mine_ref, rest_ref) = refs[:QUAD], refs[QUAD:]
    for lane, out in enumerate((mine_ref, rest_ref)):
        out[...] = (held[0][lane] + held[1][lane]) + (held[2][lane] + held[3][lane])


def both_kernel(where, mine_ref, other_ref, both_ref):
    both_ref[...] = mine_ref[...] + other_ref[...]


def before(a, b, reverse):
    return a > b if reverse else a < b


def base_kernel(near_shifts, far_shifts, counts, reverse, where, mine_ref, other_ref, *refs):
    refs = list(refs)
    lane, row, far_row = where[0], where[2], where[3]
    takes = lane == (0 if reverse else 1)
    sum_mine = jnp.where(takes, other_ref[...], 0.0)
    sum_other = jnp.where(takes, 0.0, mine_ref[...])
    near_mine = [refs.pop(0) for _ in near_shifts]
    near_other = [refs.pop(0) for _ in near_shifts]
    for df, mine, other in zip(near_shifts, near_mine, near_other):
        near_by = before(lax.rem(far_row - df + counts[1], counts[1]), far_row, reverse)
        mine, other = mine[...], other[...]
        sum_mine += jnp.where(near_by, mine, 0.0) + jnp.where(takes, other, 0.0)
        sum_other += jnp.where(near_by, other, 0.0) + jnp.where(takes, 0.0, mine)
    for dr, _ in far_shifts:
        source = lax.rem(row - dr + counts[0], counts[0])
        add = jnp.where(before(source, row, reverse), refs.pop(0)[...], 0.0)
        sum_mine, sum_other = sum_mine + add, sum_other + add
    refs[0][...], refs[1][...] = sum_mine, sum_other


def back_sum_kernel(reverse, where, mine_ref, other_ref, *refs):
    held, back = refs[:QUAD], refs[QUAD:]
    quad = where[1]
    for lane, base in enumerate((mine_ref, other_ref)):
        for o in range(QUAD):
            value = base[...]
            for i in range(QUAD):
                if i != o:
                    near_by = before(quad ^ i, quad ^ o, reverse)
                    value += jnp.where(near_by, held[i][lane], 0.0)
            back[o][lane] = value


def far_shifts_of(counts):
    shifts = [(dr, df) for dr in range(1, counts[0]) for df in range(counts[1])]
    return sorted(shifts, key=lambda shift: -sum(shift))


def carry(first, rest, reverse):
    counts = lax.axis_size("grp") // LANES, lax.axis_size("seq") // QUAD
    one, two = vmem(SHARE, HD, HD), vmem(LANES, SHARE, HD, HD)

    def swap_quad(o):
        return lambda g, s: (g, s ^ o)

    def swap_lane(g, s):
        return g ^ 1, s

    def shift(dr, df):
        return lambda g, s: (
            (g // LANES + dr) % counts[0] * LANES + g % LANES,
            (s // QUAD + df) % counts[1] * QUAD + s % QUAD,
        )

    held, inside = [None] * QUAD, [None] * QUAD
    held[ORDER[0]], inside[ORDER[0]] = first
    held[ORDER[0]] = moved(held[ORDER[0]], swap_quad(ORDER[0]))
    rest = slot_totals(ORDER[1:], reverse, *rest)
    for o in ORDER[1:]:
        held[o], inside[o] = rest[o]
        if o:
            held[o] = moved(held[o], swap_quad(o))
    mine, rest = call(sum_kernel, [one, one], [*held], 1000, grant=2)
    near_shifts, far_shifts = range(1, counts[1]), far_shifts_of(counts)
    came_mine, came_other, came_both = [], [], []
    for df in near_shifts:
        came_mine.append(moved(mine, shift(0, df)))
    other = moved(rest, swap_lane)
    for df in near_shifts:
        came_other.append(moved(other, shift(0, df)))
    both = call(both_kernel, [one], [mine, other], 1000, grant=2)[0]
    for dr, df in far_shifts:
        came_both.append(moved(both, shift(dr, df)))
    kernel = functools.partial(base_kernel, near_shifts, far_shifts, counts, reverse)
    args = [mine, other, *came_mine, *came_other, *came_both]
    sum_mine, sum_other = call(kernel, [one, one], args, 1000, grant=2)
    other = moved(sum_other, swap_lane)
    kernel = functools.partial(back_sum_kernel, reverse)
    back = call(kernel, [two] * QUAD, [sum_mine, other, *held], 1000, grant=2)
    result = [back[0]] + [None] * (QUAD - 1)
    for o in ORDER[:-1]:
        result[o] = moved(back[o], swap_quad(o))
    return result, inside


def body(queries, key_rows, value_rows, norm_gain, cotangent):
    gain = norm_gain[None, :]
    *first, keys, values = load_totals(ORDER[0], key_rows, value_rows)
    queries, cotangent = near(queries), near(cotangent)
    carried, inside = carry(first, (keys, values), False)
    attended = local_part(queries, keys, values)
    scores = turned_scores(keys, queries)
    priors, sums = [None] * QUAD, []
    for o in EARLY:
        attended, *sums, priors[o] = attended_slot(
            o, carried[o], inside[o], attended, queries, cotangent, gain, sums
        )
    late = [o for o in ORDER if o not in EARLY]
    normed, grads, late_priors, first = norm(
        late, carried, inside, attended, queries, cotangent, gain, sums
    )
    for o, prior in zip(late, late_priors):
        priors[o] = prior
    carried, later = carry(first, (queries, grads), True)
    local_v, normed = value_part(scores, grads, normed)
    grad_q = query_part(grads, values, keys, priors)
    local_k, grad_q = turned_part(values, grads, queries, grad_q)
    grad_k, grad_v = final_part(local_k, local_v, keys, values, carried, later)
    return normed, grad_q, grad_k, grad_v


def solution(mesh):
    rows = P(AXES, None)
    return jax.shard_map(
        body,
        mesh=mesh,
        in_specs=(rows, rows, rows, P(), rows),
        out_specs=(rows, rows, rows, rows),
        check_vma=False,
    )
```

```python
import functools

import jax
import jax.numpy as jnp
from jax import lax
from jax.experimental import pallas as pl
from jax.experimental.pallas import tpu as pltpu
from jax.sharding import PartitionSpec as P


H = 8
HD = 128
BLOCK = 512
EPSILON = 1e-06
AXES = ("grp", "seq")
LANES = 2
QUAD = 4
SHARE = H // (LANES * QUAD)
CUT = 256
SLAB = 256
ORDER = (3, 1, 2, 0)
EARLY = (0, 3)
UNROLL = 4
PAIR = 2
F32 = jnp.float32
BF16 = jnp.bfloat16


def mm(a, b, ca, cb):
    return lax.dot_general(a, b, (((ca,), (cb,)), ((), ())), preferred_element_type=F32)


def vmem(*shape, dtype=F32):
    return pltpu.VMEM(shape, dtype)


def near(value):
    return pltpu.with_memory_space_constraint(value, pltpu.VMEM)


def far(value):
    return pltpu.with_memory_space_constraint(value, pltpu.HBM)


def place():
    grp, seq = lax.axis_index("grp"), lax.axis_index("seq")
    return lax.rem(grp, LANES), lax.rem(seq, QUAD), lax.div(grp, LANES), lax.div(seq, QUAD)


def call(kernel, out_shape, args, flops, scratch=(), grant=8, far_in=(), far_out=(), aliases=None):
    any_space = pl.BlockSpec(memory_space=pltpu.HBM)
    near_space = pl.BlockSpec(memory_space=pltpu.VMEM)
    return pl.pallas_call(
        lambda *refs: kernel(place(), *refs),
        out_shape=out_shape,
        in_specs=[any_space if i in far_in else near_space for i in range(len(args))],
        out_specs=[any_space if i in far_out else near_space for i in range(len(out_shape))],
        scratch_shapes=scratch,
        input_output_aliases=aliases or {},
        compiler_params=pltpu.CompilerParams(vmem_limit_bytes=grant << 20),
        cost_estimate=pl.CostEstimate(flops=flops, bytes_accessed=flops // 100, transcendentals=0),
    )(*[far(a) if i in far_in else near(a) for i, a in enumerate(args)])


def head_cols(head):
    return pl.ds(pl.multiple_of(head * HD, HD), HD)


def heads_of(slot, where):
    for lane in range(LANES):
        for share in range(SHARE):
            unit = (where[0] ^ lane) * QUAD + (where[1] ^ slot)
            yield lane, share, unit * SHARE + share


def slot_block(slot, reverse, where, block, blocks, a_ref, b_ref, piece_ref, inside_ref):
    rows = pl.ds(block * BLOCK, BLOCK)
    for lane, share, head in heads_of(slot, where):
        cols = head_cols(head)
        state = mm(a_ref[rows, cols], b_ref[rows, cols], 0, 0)
        if block == (blocks - 1 if reverse else 0):
            inside_ref[block, lane, share] = jnp.zeros_like(state)
            piece_ref[lane, share] = state
        else:
            run = piece_ref[lane, share]
            inside_ref[block, lane, share] = run
            piece_ref[lane, share] = run + state


def slot_kernel(slots, reverse, where, a_ref, b_ref, *outs):
    blocks = a_ref.shape[0] // BLOCK
    for i, slot in enumerate(slots):
        for block in reversed(range(blocks)) if reverse else range(blocks):
            slot_block(slot, reverse, where, block, blocks, a_ref, b_ref, *outs[2 * i : 2 * i + 2])


def slot_shapes(blocks):
    return [vmem(LANES, SHARE, HD, HD), vmem(blocks, LANES, SHARE, HD, HD)]


def slot_totals(slots, reverse, a, b):
    tokens, features = a.shape
    outs = call(
        functools.partial(slot_kernel, slots, reverse),
        slot_shapes(tokens // BLOCK) * len(slots),
        [a, b],
        2 * tokens * features // QUAD * len(slots) * HD,
    )
    return {slot: outs[2 * i : 2 * i + 2] for i, slot in enumerate(slots)}


def first_kernel(slot, where, k_far, v_far, piece_ref, inside_ref, k_ref, v_ref, sems):
    copies = []
    for at, (_, _, head) in enumerate(heads_of(slot, where)):
        for j, (source, target) in enumerate(((k_far, k_ref), (v_far, v_ref))):
            copy = pltpu.make_async_copy(source.at[:, head_cols(head)], target.at[at], sems.at[at, j])
            copy.start()
            copies.append(copy)
    for at, (lane, share, _) in enumerate(heads_of(slot, where)):
        copies[2 * at].wait()
        copies[2 * at + 1].wait()
        run = None
        for block in range(inside_ref.shape[0]):
            rows = pl.ds(block * BLOCK, BLOCK)
            state = mm(k_ref[at, rows, :], v_ref[at, rows, :], 0, 0)
            inside_ref[block, lane, share] = jnp.zeros_like(state) if run is None else run
            run = state if run is None else run + state
        piece_ref[lane, share] = run


def first_totals(slot, keys, values):
    tokens, _ = keys.shape
    heads = LANES * SHARE
    return call(
        functools.partial(first_kernel, slot),
        slot_shapes(tokens // BLOCK),
        [keys, values],
        2 * tokens * heads * HD * HD,
        scratch=[vmem(heads, tokens, HD, dtype=BF16)] * 2 + [pltpu.SemaphoreType.DMA((heads, 2))],
        far_in=(0, 1),
    )


def triangle(size, upper=False):
    row = lax.broadcasted_iota(jnp.int32, (size, size), 0)
    col = lax.broadcasted_iota(jnp.int32, (size, size), 1)
    return row <= col if upper else row >= col


def over_units(count, step):
    def several(i, _):
        for j in range(UNROLL):
            unit = i * UNROLL + j
            step(unit // H, unit % H)
        return 0

    lax.fori_loop(0, count // UNROLL, several, 0)


def block_part(block, first, count):
    return pl.ds(pl.multiple_of(block * BLOCK + first * CUT, CUT), count * CUT)


def attend(block, cols, a_ref, b_ref, c_ref, mask, turned):
    tiles = BLOCK // CUT
    sums = [None] * tiles
    for j in range(tiles):
        first, count = (0, j + 1) if turned else (j, tiles - j)
        rows, here = block_part(block, first, count), block_part(block, j, 1)
        scores = mm(a_ref[rows, cols], b_ref[here, cols], 1, 1)
        at = (j - first) * CUT
        parts = [jnp.where(mask, scores[at : at + CUT], 0.0)]
        if at:
            parts.insert(0, scores[:at])
        if at + CUT < count * CUT:
            parts.append(scores[at + CUT :])
        scores = jnp.concatenate([part.astype(BF16) for part in parts], axis=0)
        product = mm(scores, c_ref[here, cols], 1, 0)
        for i in range(count):
            value = product[i * CUT : (i + 1) * CUT]
            sums[first + i] = value if sums[first + i] is None else sums[first + i] + value
    return sums


def local_kernel(where, q_ref, k_ref, v_ref, out_ref):
    mask = triangle(CUT)

    def step(block, head):
        cols = head_cols(head)
        sums = attend(block, cols, q_ref, k_ref, v_ref, mask, False)
        for i, value in enumerate(sums):
            out_ref[block_part(block, i, 1), cols] = value

    over_units(q_ref.shape[0] // BLOCK * H, step)


def local_part(queries, keys, values):
    tokens, features = queries.shape
    return call(
        local_kernel,
        [vmem(tokens, features)],
        [queries, keys, values],
        4 * tokens * BLOCK * features,
    )[0]


def scores_kernel(where, k_ref, q_ref, out_ref):
    mask = triangle(CUT, True)

    def step(block, head):
        cols = head_cols(head)
        for j in range(BLOCK // CUT):
            rows, here = block_part(block, 0, j + 1), block_part(block, j, 1)
            scores = mm(k_ref[rows, cols], q_ref[here, cols], 1, 1)
            to = pl.ds(j * CUT, CUT)
            out_ref[block, head, to, to] = jnp.where(mask, scores[j * CUT :], 0.0).astype(BF16)
            if j:
                out_ref[block, head, pl.ds(0, j * CUT), to] = scores[: j * CUT].astype(BF16)

    over_units(k_ref.shape[0] // BLOCK * H, step)


def turned_scores(keys, queries):
    tokens, features = keys.shape
    return call(
        scores_kernel,
        [vmem(tokens // BLOCK, H, BLOCK, BLOCK, dtype=BF16)],
        [keys, queries],
        2 * tokens * BLOCK * features,
    )[0]


def value_kernel(where, scores_ref, g_ref, ready_ref, out_ref, far_ref, sem):
    copy = pltpu.make_async_copy(ready_ref, far_ref, sem)
    copy.start()

    def step(block, head):
        cols = head_cols(head)
        tiles = BLOCK // CUT
        sums = [None] * tiles
        for j in range(tiles):
            rows = pl.ds(0, (j + 1) * CUT)
            scores = scores_ref[block, head, rows, pl.ds(j * CUT, CUT)]
            product = mm(scores, g_ref[block_part(block, j, 1), cols], 1, 0)
            for i in range(j + 1):
                value = product[i * CUT : (i + 1) * CUT]
                sums[i] = value if sums[i] is None else sums[i] + value
        for i, value in enumerate(sums):
            out_ref[block_part(block, i, 1), cols] = value

    over_units(g_ref.shape[0] // BLOCK * H, step)
    copy.wait()


def value_part(scores, grads, ready):
    tokens, features = grads.shape
    return call(
        value_kernel,
        [vmem(tokens, features), jax.ShapeDtypeStruct(ready.shape, ready.dtype)],
        [scores, grads, ready],
        2 * tokens * BLOCK * features,
        scratch=[pltpu.SemaphoreType.DMA(())],
        far_out=(1,),
    )


def attended_kernel(slot, first, where, carried_ref, inside_ref, local_ref, q_ref, dy_ref, gain_ref, *refs):
    if first:
        att_ref, square_ref, cross_ref, prior_ref = refs
    else:
        old_square, old_cross, att_ref, square_ref, cross_ref, prior_ref = refs
    blocks = q_ref.shape[0] // BLOCK
    for block in range(blocks):
        rows = pl.ds(block * BLOCK, BLOCK)
        square = None if first else old_square[rows, :]
        cross = None if first else old_cross[rows, :]
        for lane, share, head in heads_of(slot, where):
            cols = head_cols(head)
            prior = (carried_ref[lane, share] + inside_ref[block, lane, share]).astype(BF16)
            prior_ref[block, lane, share] = prior
            att = local_ref[rows, cols] + mm(q_ref[rows, cols], prior, 1, 0)
            att_ref[rows, cols] = att
            term = dy_ref[rows, cols].astype(F32) * gain_ref[:, cols] * att
            square = att * att if square is None else square + att * att
            cross = term if cross is None else cross + term
        square_ref[rows, :] = square
        cross_ref[rows, :] = cross


def attended_slot(slot, carried, inside, local, queries, cotangent, gain, sums):
    tokens, features = queries.shape
    blocks = tokens // BLOCK
    first = not sums
    return call(
        functools.partial(attended_kernel, slot, first),
        [vmem(tokens, features), vmem(tokens, HD), vmem(tokens, HD)]
        + [vmem(blocks, LANES, SHARE, HD, HD, dtype=BF16)],
        [carried, inside, local, queries, cotangent, gain, *sums],
        2 * tokens * features // QUAD * HD,
        aliases={2: 0},
    )


def norm_kernel(slots, where, *refs):
    count = len(slots)
    carried, inside = refs[:count], refs[count : 2 * count]
    local_ref, q_ref, dy_ref, gain_ref, old_square, old_cross = refs[2 * count : 2 * count + 6]
    outs = refs[2 * count + 6 :]
    att_ref, out_ref, grad_ref = outs[:3]
    priors, (piece_ref, later_ref, square_ref, cross_ref) = outs[3 : 3 + count], outs[3 + count :]
    blocks = q_ref.shape[0] // BLOCK
    features = H * HD
    for block in reversed(range(blocks)):
        rows = pl.ds(block * BLOCK, BLOCK)
        square, cross = old_square[rows, :], old_cross[rows, :]
        for i, slot in enumerate(slots):
            for lane, share, head in heads_of(slot, where):
                cols = head_cols(head)
                prior = (carried[i][lane, share] + inside[i][block, lane, share]).astype(BF16)
                priors[i][block, lane, share] = prior
                att = local_ref[rows, cols] + mm(q_ref[rows, cols], prior, 1, 0)
                att_ref[rows, cols] = att
                square += att * att
                cross += dy_ref[rows, cols].astype(F32) * gain_ref[:, cols] * att
        square_ref[...], cross_ref[...] = square, cross

        def step(i, _):
            here = pl.ds(pl.multiple_of(i * SLAB, SLAB), SLAB)
            rows = pl.ds(pl.multiple_of(block * BLOCK + i * SLAB, SLAB), SLAB)
            square = jnp.sum(square_ref[here, :], axis=1, keepdims=True) / features
            inverse = lax.rsqrt(square + EPSILON)
            mean = inverse * (jnp.sum(cross_ref[here, :], axis=1, keepdims=True) / features)
            for head in range(H):
                cols = pl.ds(head * HD, HD)
                unit = att_ref[rows, cols] * inverse
                gain = gain_ref[:, cols]
                out_ref[rows, cols] = (unit * gain).astype(BF16)
                scaled = dy_ref[rows, cols].astype(F32) * gain
                grad_ref[rows, cols] = (inverse * (scaled - unit * mean)).astype(BF16)
            return 0

        lax.fori_loop(0, BLOCK // SLAB, step, 0)
        slot_block(ORDER[0], True, where, block, blocks, q_ref, grad_ref, piece_ref, later_ref)


def norm(slots, carried, inside, attended, queries, cotangent, gain, sums):
    tokens, features = attended.shape
    blocks = tokens // BLOCK
    half = vmem(tokens, features, dtype=BF16)
    prior = vmem(blocks, LANES, SHARE, HD, HD, dtype=BF16)
    carried, inside = [carried[o] for o in slots], [inside[o] for o in slots]
    _, normed, grads, *outs = call(
        functools.partial(norm_kernel, slots),
        [vmem(tokens, features), half, half] + [prior] * len(slots) + slot_shapes(blocks),
        [*carried, *inside, attended, queries, cotangent, gain, *sums],
        20 * tokens * features,
        scratch=[vmem(BLOCK, HD)] * 2,
        aliases={2 * len(slots): 0},
    )
    return normed, grads, outs[: len(slots)], outs[len(slots) :]


def query_kernel(where, g_ref, v_ref, k_ref, *refs):
    priors, (out_ref, prior_ref) = refs[:QUAD], refs[QUAD:]
    mask = triangle(CUT)
    prior_ref[...] = jnp.zeros_like(prior_ref)
    for slot in range(QUAD):
        for lane, share, head in heads_of(slot, where):
            cols = head_cols(head % PAIR)
            for block in range(prior_ref.shape[0]):
                prior_ref[block, head // PAIR, cols, cols] = priors[slot][block, lane, share]

    def step(block, pair):
        wide = pl.ds(pl.multiple_of(pair * PAIR * HD, PAIR * HD), PAIR * HD)
        rows = block_part(block, 0, BLOCK // CUT)
        far_part = mm(g_ref[rows, wide], prior_ref[block, pair], 1, 1)
        for j in range(PAIR):
            cols = head_cols(pair * PAIR + j)
            sums = attend(block, cols, g_ref, v_ref, k_ref, mask, False)
            for i, value in enumerate(sums):
                value += far_part[i * CUT : (i + 1) * CUT, j * HD : (j + 1) * HD]
                out_ref[block_part(block, i, 1), cols] = value.astype(BF16)

    def several(i, _):
        for j in range(UNROLL // PAIR):
            unit = i * (UNROLL // PAIR) + j
            step(unit // (H // PAIR), unit % (H // PAIR))
        return 0

    lax.fori_loop(0, g_ref.shape[0] // BLOCK * H // UNROLL, several, 0)


def query_part(grads, values, keys, priors):
    tokens, features = grads.shape
    return call(
        query_kernel,
        [vmem(tokens, features, dtype=BF16)],
        [grads, values, keys, *priors],
        4 * tokens * BLOCK * features,
        scratch=[vmem(tokens // BLOCK, H // PAIR, PAIR * HD, PAIR * HD, dtype=BF16)],
    )[0]


def turned_kernel(where, a_ref, b_ref, c_ref, ready_ref, out_ref, far_ref, sem):
    copy = pltpu.make_async_copy(ready_ref, far_ref, sem)
    copy.start()
    mask = triangle(CUT, True)

    def step(block, head):
        cols = head_cols(head)
        sums = attend(block, cols, a_ref, b_ref, c_ref, mask, True)
        for i, value in enumerate(sums):
            out_ref[block_part(block, i, 1), cols] = value

    over_units(a_ref.shape[0] // BLOCK * H, step)
    copy.wait()


def turned_part(a, b, c, ready):
    tokens, features = a.shape
    return call(
        turned_kernel,
        [vmem(tokens, features), jax.ShapeDtypeStruct(ready.shape, ready.dtype)],
        [a, b, c, ready],
        4 * tokens * BLOCK * features,
        scratch=[pltpu.SemaphoreType.DMA(())],
        far_out=(1,),
    )


def final_kernel(slots, where, lk_ref, lv_ref, k_ref, v_ref, *refs):
    count = len(slots)
    carried, later = refs[:count], refs[count : 2 * count]
    gk_far, gv_far, gk_ref, gv_ref, sems = refs[-5:]
    copies = []
    for i, slot in enumerate(slots):
        for lane, share, head in heads_of(slot, where):
            cols, at = head_cols(head), len(copies) // 2
            for block in range(k_ref.shape[0] // BLOCK):
                rows = pl.ds(block * BLOCK, BLOCK)
                state = (carried[i][lane, share] + later[i][block, lane, share]).astype(BF16)
                grad_k = lk_ref[rows, cols] + mm(v_ref[rows, cols], state, 1, 1)
                grad_v = lv_ref[rows, cols] + mm(k_ref[rows, cols], state, 1, 0)
                gk_ref[at, rows, :], gv_ref[at, rows, :] = grad_k.astype(BF16), grad_v.astype(BF16)
            for j, (source, target) in enumerate(((gk_ref, gk_far), (gv_ref, gv_far))):
                copy = pltpu.make_async_copy(source.at[at], target.at[:, cols], sems.at[at, j])
                copy.start()
                copies.append(copy)
    for copy in copies:
        copy.wait()


def final_part(slots, local_k, local_v, keys, values, carried, later, made=()):
    tokens, features = keys.shape
    heads = len(slots) * LANES * SHARE
    args = [local_k, local_v, keys, values]
    args += [carried[o] for o in slots] + [later[o] for o in slots]
    places = range(len(args), len(args) + len(made))
    return call(
        functools.partial(final_kernel, slots),
        [jax.ShapeDtypeStruct((tokens, features), BF16)] * 2,
        [*args, *made],
        4 * tokens * heads * HD * HD,
        scratch=[vmem(heads, tokens, HD, dtype=BF16)] * 2 + [pltpu.SemaphoreType.DMA((heads, 2))],
        far_in=places,
        far_out=(0, 1),
        grant=12,
        aliases={place: i for i, place in enumerate(places)},
    )


def moved(value, move):
    groups, shards = lax.axis_size("grp"), lax.axis_size("seq")
    pairs = []
    for g in range(groups):
        for s in range(shards):
            to_g, to_s = move(g, s)
            pairs.append((g * shards + s, to_g * shards + to_s))
    return lax.ppermute(value, AXES, pairs)


def sum_kernel(where, *refs):
    held, (mine_ref, rest_ref) = refs[:QUAD], refs[QUAD:]
    for lane, out in enumerate((mine_ref, rest_ref)):
        out[...] = (held[0][lane] + held[1][lane]) + (held[2][lane] + held[3][lane])


def both_kernel(where, mine_ref, other_ref, both_ref):
    both_ref[...] = mine_ref[...] + other_ref[...]


def before(a, b, reverse):
    return a > b if reverse else a < b


def base_kernel(near_shifts, far_shifts, counts, reverse, where, mine_ref, other_ref, *refs):
    refs = list(refs)
    lane, row, far_row = where[0], where[2], where[3]
    takes = lane == (0 if reverse else 1)
    sum_mine = jnp.where(takes, other_ref[...], 0.0)
    sum_other = jnp.where(takes, 0.0, mine_ref[...])
    near_mine = [refs.pop(0) for _ in near_shifts]
    near_other = [refs.pop(0) for _ in near_shifts]
    for df, mine, other in zip(near_shifts, near_mine, near_other):
        near_by = before(lax.rem(far_row - df + counts[1], counts[1]), far_row, reverse)
        mine, other = mine[...], other[...]
        sum_mine += jnp.where(near_by, mine, 0.0) + jnp.where(takes, other, 0.0)
        sum_other += jnp.where(near_by, other, 0.0) + jnp.where(takes, 0.0, mine)
    for dr, _ in far_shifts:
        source = lax.rem(row - dr + counts[0], counts[0])
        add = jnp.where(before(source, row, reverse), refs.pop(0)[...], 0.0)
        sum_mine, sum_other = sum_mine + add, sum_other + add
    refs[0][...], refs[1][...] = sum_mine, sum_other


def back_sum_kernel(reverse, where, mine_ref, other_ref, *refs):
    held, back = refs[:QUAD], refs[QUAD:]
    quad = where[1]
    for lane, base in enumerate((mine_ref, other_ref)):
        for o in range(QUAD):
            value = base[...]
            for i in range(QUAD):
                if i != o:
                    near_by = before(quad ^ i, quad ^ o, reverse)
                    value += jnp.where(near_by, held[i][lane], 0.0)
            back[o][lane] = value


def far_shifts_of(counts):
    shifts = [(dr, df) for dr in range(1, counts[0]) for df in range(counts[1])]
    return sorted(shifts, key=lambda shift: -sum(shift))


def carry(first, rest, reverse):
    counts = lax.axis_size("grp") // LANES, lax.axis_size("seq") // QUAD
    one, two = vmem(SHARE, HD, HD), vmem(LANES, SHARE, HD, HD)

    def swap_quad(o):
        return lambda g, s: (g, s ^ o)

    def swap_lane(g, s):
        return g ^ 1, s

    def shift(dr, df):
        return lambda g, s: (
            (g // LANES + dr) % counts[0] * LANES + g % LANES,
            (s // QUAD + df) % counts[1] * QUAD + s % QUAD,
        )

    held, inside = [None] * QUAD, [None] * QUAD
    held[ORDER[0]], inside[ORDER[0]] = first
    held[ORDER[0]] = moved(held[ORDER[0]], swap_quad(ORDER[0]))
    rest = slot_totals(ORDER[1:], reverse, *rest)
    for o in ORDER[1:]:
        held[o], inside[o] = rest[o]
        if o:
            held[o] = moved(held[o], swap_quad(o))
    mine, rest = call(sum_kernel, [one, one], [*held], 1000, grant=2)
    near_shifts, far_shifts = range(1, counts[1]), far_shifts_of(counts)
    came_mine, came_other, came_both = [], [], []
    for df in near_shifts:
        came_mine.append(moved(mine, shift(0, df)))
    other = moved(rest, swap_lane)
    for df in near_shifts:
        came_other.append(moved(other, shift(0, df)))
    both = call(both_kernel, [one], [mine, other], 1000, grant=2)[0]
    for dr, df in far_shifts:
        came_both.append(moved(both, shift(dr, df)))
    kernel = functools.partial(base_kernel, near_shifts, far_shifts, counts, reverse)
    args = [mine, other, *came_mine, *came_other, *came_both]
    sum_mine, sum_other = call(kernel, [one, one], args, 1000, grant=2)
    other = moved(sum_other, swap_lane)
    kernel = functools.partial(back_sum_kernel, reverse)
    back = call(kernel, [two] * QUAD, [sum_mine, other, *held], 1000, grant=2)
    result = [back[0]] + [None] * (QUAD - 1)
    for o in ORDER[:-1]:
        result[o] = moved(back[o], swap_quad(o))
    return result, inside


def body(queries, key_rows, value_rows, norm_gain, cotangent):
    gain = norm_gain[None, :]
    first = first_totals(ORDER[0], key_rows, value_rows)
    keys, values, queries, cotangent = (near(a) for a in (key_rows, value_rows, queries, cotangent))
    carried, inside = carry(first, (keys, values), False)
    attended = local_part(queries, keys, values)
    scores = turned_scores(keys, queries)
    priors, sums = [None] * QUAD, []
    for o in EARLY:
        attended, *sums, priors[o] = attended_slot(
            o, carried[o], inside[o], attended, queries, cotangent, gain, sums
        )
    late = [o for o in ORDER if o not in EARLY]
    normed, grads, late_priors, first = norm(
        late, carried, inside, attended, queries, cotangent, gain, sums
    )
    for o, prior in zip(late, late_priors):
        priors[o] = prior
    carried, later = carry(first, (queries, grads), True)
    local_v, normed = value_part(scores, grads, normed)
    grad_q = query_part(grads, values, keys, priors)
    local_k, grad_q = turned_part(values, grads, queries, grad_q)
    args = local_k, local_v, keys, values, carried, later
    made = final_part((0,), *args)
    grad_k, grad_v = final_part(ORDER[:-1], *args, made)
    return normed, grad_q, grad_k, grad_v


def solution(mesh):
    rows = P(AXES, None)
    return jax.shard_map(
        body,
        mesh=mesh,
        in_specs=(rows, rows, rows, P(), rows),
        out_specs=(rows, rows, rows, rows),
        check_vma=False,
    )
```

```python
import functools

import jax
import jax.numpy as jnp
from jax import lax
from jax.experimental import pallas as pl
from jax.experimental.pallas import tpu as pltpu
from jax.sharding import PartitionSpec as P


H = 8
HD = 128
BLOCK = 512
EPSILON = 1e-06
AXES = ("grp", "seq")
LANES = 2
QUAD = 4
SHARE = H // (LANES * QUAD)
CUT = 256
SLAB = 512
ORDER = (3, 1, 2, 0)
EARLY = (0, 3)
UNROLL = 8
PAIR = 2
F32 = jnp.float32
BF16 = jnp.bfloat16


def mm(a, b, ca, cb):
    return lax.dot_general(a, b, (((ca,), (cb,)), ((), ())), preferred_element_type=F32)


def vmem(*shape, dtype=F32):
    return pltpu.VMEM(shape, dtype)


def near(value):
    return pltpu.with_memory_space_constraint(value, pltpu.VMEM)


def far(value):
    return pltpu.with_memory_space_constraint(value, pltpu.HBM)


def place():
    grp, seq = lax.axis_index("grp"), lax.axis_index("seq")
    return lax.rem(grp, LANES), lax.rem(seq, QUAD), lax.div(grp, LANES), lax.div(seq, QUAD)


def call(kernel, out_shape, args, flops, scratch=(), grant=8, far_in=(), far_out=(), aliases=None):
    any_space = pl.BlockSpec(memory_space=pltpu.HBM)
    near_space = pl.BlockSpec(memory_space=pltpu.VMEM)
    return pl.pallas_call(
        lambda *refs: kernel(place(), *refs),
        out_shape=out_shape,
        in_specs=[any_space if i in far_in else near_space for i in range(len(args))],
        out_specs=[any_space if i in far_out else near_space for i in range(len(out_shape))],
        scratch_shapes=scratch,
        input_output_aliases=aliases or {},
        compiler_params=pltpu.CompilerParams(vmem_limit_bytes=grant << 20),
        cost_estimate=pl.CostEstimate(flops=flops, bytes_accessed=flops // 100, transcendentals=0),
    )(*[far(a) if i in far_in else near(a) for i, a in enumerate(args)])


def head_cols(head):
    return pl.ds(pl.multiple_of(head * HD, HD), HD)


def heads_of(slot, where):
    for lane in range(LANES):
        for share in range(SHARE):
            unit = (where[0] ^ lane) * QUAD + (where[1] ^ slot)
            yield lane, share, unit * SHARE + share


def slot_block(slot, reverse, where, block, blocks, a_ref, b_ref, piece_ref, inside_ref):
    rows = pl.ds(block * BLOCK, BLOCK)
    for lane, share, head in heads_of(slot, where):
        cols = head_cols(head)
        state = mm(a_ref[rows, cols], b_ref[rows, cols], 0, 0)
        if block == (blocks - 1 if reverse else 0):
            inside_ref[block, lane, share] = jnp.zeros_like(state)
            piece_ref[lane, share] = state
        else:
            run = piece_ref[lane, share]
            inside_ref[block, lane, share] = run
            piece_ref[lane, share] = run + state


def slot_kernel(slots, reverse, where, a_ref, b_ref, *outs):
    blocks = a_ref.shape[0] // BLOCK
    for i, slot in enumerate(slots):
        for block in reversed(range(blocks)) if reverse else range(blocks):
            slot_block(slot, reverse, where, block, blocks, a_ref, b_ref, *outs[2 * i : 2 * i + 2])


def slot_shapes(blocks):
    return [vmem(LANES, SHARE, HD, HD), vmem(blocks, LANES, SHARE, HD, HD)]


def slot_totals(slots, reverse, a, b):
    tokens, features = a.shape
    outs = call(
        functools.partial(slot_kernel, slots, reverse),
        slot_shapes(tokens // BLOCK) * len(slots),
        [a, b],
        2 * tokens * features // QUAD * len(slots) * HD,
    )
    return {slot: outs[2 * i : 2 * i + 2] for i, slot in enumerate(slots)}


def first_kernel(slot, where, k_far, v_far, piece_ref, inside_ref, k_ref, v_ref, sems):
    copies = []
    for at, (_, _, head) in enumerate(heads_of(slot, where)):
        for j, (source, target) in enumerate(((k_far, k_ref), (v_far, v_ref))):
            copy = pltpu.make_async_copy(source.at[:, head_cols(head)], target.at[at], sems.at[at, j])
            copy.start()
            copies.append(copy)
    for at, (lane, share, _) in enumerate(heads_of(slot, where)):
        copies[2 * at].wait()
        copies[2 * at + 1].wait()
        run = None
        for block in range(inside_ref.shape[0]):
            rows = pl.ds(block * BLOCK, BLOCK)
            state = mm(k_ref[at, rows, :], v_ref[at, rows, :], 0, 0)
            inside_ref[block, lane, share] = jnp.zeros_like(state) if run is None else run
            run = state if run is None else run + state
        piece_ref[lane, share] = run


def first_totals(slot, keys, values):
    tokens, _ = keys.shape
    heads = LANES * SHARE
    return call(
        functools.partial(first_kernel, slot),
        slot_shapes(tokens // BLOCK),
        [keys, values],
        2 * tokens * heads * HD * HD,
        scratch=[vmem(heads, tokens, HD, dtype=BF16)] * 2 + [pltpu.SemaphoreType.DMA((heads, 2))],
        far_in=(0, 1),
    )


def triangle(size, upper=False):
    row = lax.broadcasted_iota(jnp.int32, (size, size), 0)
    col = lax.broadcasted_iota(jnp.int32, (size, size), 1)
    return row <= col if upper else row >= col


def over_units(count, step):
    def several(i, _):
        for j in range(UNROLL):
            unit = i * UNROLL + j
            step(unit // H, unit % H)
        return 0

    lax.fori_loop(0, count // UNROLL, several, 0)


def block_part(block, first, count):
    return pl.ds(pl.multiple_of(block * BLOCK + first * CUT, CUT), count * CUT)


def attend(block, cols, a_ref, b_ref, c_ref, mask, turned):
    tiles = BLOCK // CUT
    sums = [None] * tiles
    for j in range(tiles):
        first, count = (0, j + 1) if turned else (j, tiles - j)
        rows, here = block_part(block, first, count), block_part(block, j, 1)
        scores = mm(a_ref[rows, cols], b_ref[here, cols], 1, 1)
        at = (j - first) * CUT
        parts = [jnp.where(mask, scores[at : at + CUT], 0.0)]
        if at:
            parts.insert(0, scores[:at])
        if at + CUT < count * CUT:
            parts.append(scores[at + CUT :])
        scores = jnp.concatenate([part.astype(BF16) for part in parts], axis=0)
        product = mm(scores, c_ref[here, cols], 1, 0)
        for i in range(count):
            value = product[i * CUT : (i + 1) * CUT]
            sums[first + i] = value if sums[first + i] is None else sums[first + i] + value
    return sums


def local_kernel(where, q_ref, k_ref, v_ref, out_ref):
    mask = triangle(CUT)

    def step(block, head):
        cols = head_cols(head)
        sums = attend(block, cols, q_ref, k_ref, v_ref, mask, False)
        for i, value in enumerate(sums):
            out_ref[block_part(block, i, 1), cols] = value

    over_units(q_ref.shape[0] // BLOCK * H, step)


def local_part(queries, keys, values):
    tokens, features = queries.shape
    return call(
        local_kernel,
        [vmem(tokens, features)],
        [queries, keys, values],
        4 * tokens * BLOCK * features,
    )[0]


def scores_kernel(where, k_ref, q_ref, out_ref):
    mask = triangle(CUT, True)

    def step(block, head):
        cols = head_cols(head)
        for j in range(BLOCK // CUT):
            rows, here = block_part(block, 0, j + 1), block_part(block, j, 1)
            scores = mm(k_ref[rows, cols], q_ref[here, cols], 1, 1)
            to = pl.ds(j * CUT, CUT)
            out_ref[block, head, to, to] = jnp.where(mask, scores[j * CUT :], 0.0).astype(BF16)
            if j:
                out_ref[block, head, pl.ds(0, j * CUT), to] = scores[: j * CUT].astype(BF16)

    over_units(k_ref.shape[0] // BLOCK * H, step)


def turned_scores(keys, queries):
    tokens, features = keys.shape
    return call(
        scores_kernel,
        [vmem(tokens // BLOCK, H, BLOCK, BLOCK, dtype=BF16)],
        [keys, queries],
        2 * tokens * BLOCK * features,
    )[0]


def value_kernel(where, scores_ref, g_ref, ready_ref, out_ref, far_ref, sem):
    copy = pltpu.make_async_copy(ready_ref, far_ref, sem)
    copy.start()

    def step(block, head):
        cols = head_cols(head)
        tiles = BLOCK // CUT
        sums = [None] * tiles
        for j in range(tiles):
            rows = pl.ds(0, (j + 1) * CUT)
            scores = scores_ref[block, head, rows, pl.ds(j * CUT, CUT)]
            product = mm(scores, g_ref[block_part(block, j, 1), cols], 1, 0)
            for i in range(j + 1):
                value = product[i * CUT : (i + 1) * CUT]
                sums[i] = value if sums[i] is None else sums[i] + value
        for i, value in enumerate(sums):
            out_ref[block_part(block, i, 1), cols] = value

    over_units(g_ref.shape[0] // BLOCK * H, step)
    copy.wait()


def value_part(scores, grads, ready):
    tokens, features = grads.shape
    return call(
        value_kernel,
        [vmem(tokens, features), jax.ShapeDtypeStruct(ready.shape, ready.dtype)],
        [scores, grads, ready],
        2 * tokens * BLOCK * features,
        scratch=[pltpu.SemaphoreType.DMA(())],
        far_out=(1,),
    )


def attended_kernel(slot, first, where, carried_ref, inside_ref, local_ref, q_ref, dy_ref, gain_ref, *refs):
    if first:
        att_ref, square_ref, cross_ref, prior_ref = refs
    else:
        old_square, old_cross, att_ref, square_ref, cross_ref, prior_ref = refs
    blocks = q_ref.shape[0] // BLOCK
    for block in range(blocks):
        rows = pl.ds(block * BLOCK, BLOCK)
        square = None if first else old_square[rows, :]
        cross = None if first else old_cross[rows, :]
        for lane, share, head in heads_of(slot, where):
            cols = head_cols(head)
            prior = (carried_ref[lane, share] + inside_ref[block, lane, share]).astype(BF16)
            prior_ref[block, lane, share] = prior
            att = local_ref[rows, cols] + mm(q_ref[rows, cols], prior, 1, 0)
            att_ref[rows, cols] = att
            term = dy_ref[rows, cols].astype(F32) * gain_ref[:, cols] * att
            square = att * att if square is None else square + att * att
            cross = term if cross is None else cross + term
        square_ref[rows, :] = square
        cross_ref[rows, :] = cross


def attended_slot(slot, carried, inside, local, queries, cotangent, gain, sums):
    tokens, features = queries.shape
    blocks = tokens // BLOCK
    first = not sums
    return call(
        functools.partial(attended_kernel, slot, first),
        [vmem(tokens, features), vmem(tokens, HD), vmem(tokens, HD)]
        + [vmem(blocks, LANES, SHARE, HD, HD, dtype=BF16)],
        [carried, inside, local, queries, cotangent, gain, *sums],
        2 * tokens * features // QUAD * HD,
        aliases={2: 0},
    )


def norm_kernel(slots, where, *refs):
    count = len(slots)
    carried, inside = refs[:count], refs[count : 2 * count]
    local_ref, q_ref, dy_ref, gain_ref, old_square, old_cross = refs[2 * count : 2 * count + 6]
    outs = refs[2 * count + 6 :]
    att_ref, out_ref, grad_ref = outs[:3]
    priors, (piece_ref, later_ref, square_ref, cross_ref) = outs[3 : 3 + count], outs[3 + count :]
    blocks = q_ref.shape[0] // BLOCK
    features = H * HD
    for block in reversed(range(blocks)):
        rows = pl.ds(block * BLOCK, BLOCK)
        square, cross = old_square[rows, :], old_cross[rows, :]
        for i, slot in enumerate(slots):
            for lane, share, head in heads_of(slot, where):
                cols = head_cols(head)
                prior = (carried[i][lane, share] + inside[i][block, lane, share]).astype(BF16)
                priors[i][block, lane, share] = prior
                att = local_ref[rows, cols] + mm(q_ref[rows, cols], prior, 1, 0)
                att_ref[rows, cols] = att
                square += att * att
                cross += dy_ref[rows, cols].astype(F32) * gain_ref[:, cols] * att
        square_ref[...], cross_ref[...] = square, cross

        def step(i, _):
            here = pl.ds(pl.multiple_of(i * SLAB, SLAB), SLAB)
            rows = pl.ds(pl.multiple_of(block * BLOCK + i * SLAB, SLAB), SLAB)
            square = jnp.sum(square_ref[here, :], axis=1, keepdims=True) / features
            inverse = lax.rsqrt(square + EPSILON)
            mean = inverse * (jnp.sum(cross_ref[here, :], axis=1, keepdims=True) / features)
            weight = inverse * inverse * mean
            inverse, weight = (jnp.broadcast_to(x, (SLAB, HD)) for x in (inverse, weight))
            for head in range(H):
                cols = pl.ds(head * HD, HD)
                att = att_ref[rows, cols]
                gain = gain_ref[:, cols] * inverse
                out_ref[rows, cols] = (att * gain).astype(BF16)
                scaled = dy_ref[rows, cols].astype(F32) * gain
                grad_ref[rows, cols] = (scaled - att * weight).astype(BF16)
            return 0

        lax.fori_loop(0, BLOCK // SLAB, step, 0)
        slot_block(ORDER[0], True, where, block, blocks, q_ref, grad_ref, piece_ref, later_ref)


def norm(slots, carried, inside, attended, queries, cotangent, gain, sums):
    tokens, features = attended.shape
    blocks = tokens // BLOCK
    half = vmem(tokens, features, dtype=BF16)
    prior = vmem(blocks, LANES, SHARE, HD, HD, dtype=BF16)
    carried, inside = [carried[o] for o in slots], [inside[o] for o in slots]
    _, normed, grads, *outs = call(
        functools.partial(norm_kernel, slots),
        [vmem(tokens, features), half, half] + [prior] * len(slots) + slot_shapes(blocks),
        [*carried, *inside, attended, queries, cotangent, gain, *sums],
        20 * tokens * features,
        scratch=[vmem(BLOCK, HD)] * 2,
        aliases={2 * len(slots): 0},
    )
    return normed, grads, outs[: len(slots)], outs[len(slots) :]


def query_kernel(where, g_ref, v_ref, k_ref, *refs):
    priors, (out_ref, prior_ref) = refs[:QUAD], refs[QUAD:]
    mask = triangle(CUT)
    prior_ref[...] = jnp.zeros_like(prior_ref)
    for slot in range(QUAD):
        for lane, share, head in heads_of(slot, where):
            cols = head_cols(head % PAIR)
            for block in range(prior_ref.shape[0]):
                prior_ref[block, head // PAIR, cols, cols] = priors[slot][block, lane, share]

    def step(block, pair):
        wide = pl.ds(pl.multiple_of(pair * PAIR * HD, PAIR * HD), PAIR * HD)
        rows = block_part(block, 0, BLOCK // CUT)
        far_part = mm(g_ref[rows, wide], prior_ref[block, pair], 1, 1)
        for j in range(PAIR):
            cols = head_cols(pair * PAIR + j)
            sums = attend(block, cols, g_ref, v_ref, k_ref, mask, False)
            for i, value in enumerate(sums):
                value += far_part[i * CUT : (i + 1) * CUT, j * HD : (j + 1) * HD]
                out_ref[block_part(block, i, 1), cols] = value.astype(BF16)

    def several(i, _):
        for j in range(UNROLL // PAIR):
            unit = i * (UNROLL // PAIR) + j
            step(unit // (H // PAIR), unit % (H // PAIR))
        return 0

    lax.fori_loop(0, g_ref.shape[0] // BLOCK * H // UNROLL, several, 0)


def query_part(grads, values, keys, priors):
    tokens, features = grads.shape
    return call(
        query_kernel,
        [vmem(tokens, features, dtype=BF16)],
        [grads, values, keys, *priors],
        4 * tokens * BLOCK * features,
        scratch=[vmem(tokens // BLOCK, H // PAIR, PAIR * HD, PAIR * HD, dtype=BF16)],
    )[0]


def turned_kernel(where, a_ref, b_ref, c_ref, ready_ref, out_ref, far_ref, sem):
    copy = pltpu.make_async_copy(ready_ref, far_ref, sem)
    copy.start()
    mask = triangle(CUT, True)

    def step(block, head):
        cols = head_cols(head)
        sums = attend(block, cols, a_ref, b_ref, c_ref, mask, True)
        for i, value in enumerate(sums):
            out_ref[block_part(block, i, 1), cols] = value

    over_units(a_ref.shape[0] // BLOCK * H, step)
    copy.wait()


def turned_part(a, b, c, ready):
    tokens, features = a.shape
    return call(
        turned_kernel,
        [vmem(tokens, features), jax.ShapeDtypeStruct(ready.shape, ready.dtype)],
        [a, b, c, ready],
        4 * tokens * BLOCK * features,
        scratch=[pltpu.SemaphoreType.DMA(())],
        far_out=(1,),
    )


def final_kernel(slots, where, lk_ref, lv_ref, k_ref, v_ref, *refs):
    count = len(slots)
    carried, later = refs[:count], refs[count : 2 * count]
    gk_far, gv_far, gk_ref, gv_ref, sems = refs[-5:]
    copies = []
    for i, slot in enumerate(slots):
        for lane, share, head in heads_of(slot, where):
            cols, at = head_cols(head), len(copies) // 2
            for block in range(k_ref.shape[0] // BLOCK):
                rows = pl.ds(block * BLOCK, BLOCK)
                state = (carried[i][lane, share] + later[i][block, lane, share]).astype(BF16)
                grad_k = lk_ref[rows, cols] + mm(v_ref[rows, cols], state, 1, 1)
                grad_v = lv_ref[rows, cols] + mm(k_ref[rows, cols], state, 1, 0)
                gk_ref[at, rows, :], gv_ref[at, rows, :] = grad_k.astype(BF16), grad_v.astype(BF16)
            for j, (source, target) in enumerate(((gk_ref, gk_far), (gv_ref, gv_far))):
                copy = pltpu.make_async_copy(source.at[at], target.at[:, cols], sems.at[at, j])
                copy.start()
                copies.append(copy)
    for copy in copies:
        copy.wait()


def final_part(slots, local_k, local_v, keys, values, carried, later, made=()):
    tokens, features = keys.shape
    heads = len(slots) * LANES * SHARE
    args = [local_k, local_v, keys, values]
    args += [carried[o] for o in slots] + [later[o] for o in slots]
    places = range(len(args), len(args) + len(made))
    return call(
        functools.partial(final_kernel, slots),
        [jax.ShapeDtypeStruct((tokens, features), BF16)] * 2,
        [*args, *made],
        4 * tokens * heads * HD * HD,
        scratch=[vmem(heads, tokens, HD, dtype=BF16)] * 2 + [pltpu.SemaphoreType.DMA((heads, 2))],
        far_in=places,
        far_out=(0, 1),
        grant=12,
        aliases={place: i for i, place in enumerate(places)},
    )


def moved(value, move):
    groups, shards = lax.axis_size("grp"), lax.axis_size("seq")
    pairs = []
    for g in range(groups):
        for s in range(shards):
            to_g, to_s = move(g, s)
            pairs.append((g * shards + s, to_g * shards + to_s))
    return lax.ppermute(value, AXES, pairs)


def sum_kernel(where, *refs):
    held, (mine_ref, rest_ref) = refs[:QUAD], refs[QUAD:]
    for lane, out in enumerate((mine_ref, rest_ref)):
        out[...] = (held[0][lane] + held[1][lane]) + (held[2][lane] + held[3][lane])


def both_kernel(where, mine_ref, other_ref, both_ref):
    both_ref[...] = mine_ref[...] + other_ref[...]


def before(a, b, reverse):
    return a > b if reverse else a < b


def base_kernel(near_shifts, far_shifts, counts, reverse, where, mine_ref, other_ref, *refs):
    refs = list(refs)
    lane, row, far_row = where[0], where[2], where[3]
    takes = lane == (0 if reverse else 1)
    sum_mine = jnp.where(takes, other_ref[...], 0.0)
    sum_other = jnp.where(takes, 0.0, mine_ref[...])
    near_mine = [refs.pop(0) for _ in near_shifts]
    near_other = [refs.pop(0) for _ in near_shifts]
    for df, mine, other in zip(near_shifts, near_mine, near_other):
        near_by = before(lax.rem(far_row - df + counts[1], counts[1]), far_row, reverse)
        mine, other = mine[...], other[...]
        sum_mine += jnp.where(near_by, mine, 0.0) + jnp.where(takes, other, 0.0)
        sum_other += jnp.where(near_by, other, 0.0) + jnp.where(takes, 0.0, mine)
    for dr, _ in far_shifts:
        source = lax.rem(row - dr + counts[0], counts[0])
        add = jnp.where(before(source, row, reverse), refs.pop(0)[...], 0.0)
        sum_mine, sum_other = sum_mine + add, sum_other + add
    refs[0][...], refs[1][...] = sum_mine, sum_other


def back_sum_kernel(reverse, where, mine_ref, other_ref, *refs):
    held, back = refs[:QUAD], refs[QUAD:]
    quad = where[1]
    for lane, base in enumerate((mine_ref, other_ref)):
        for o in range(QUAD):
            value = base[...]
            for i in range(QUAD):
                if i != o:
                    near_by = before(quad ^ i, quad ^ o, reverse)
                    value += jnp.where(near_by, held[i][lane], 0.0)
            back[o][lane] = value


def far_shifts_of(counts):
    shifts = [(dr, df) for dr in range(1, counts[0]) for df in range(counts[1])]
    return sorted(shifts, key=lambda shift: -sum(shift))


def carry(first, rest, reverse):
    counts = lax.axis_size("grp") // LANES, lax.axis_size("seq") // QUAD
    one, two = vmem(SHARE, HD, HD), vmem(LANES, SHARE, HD, HD)

    def swap_quad(o):
        return lambda g, s: (g, s ^ o)

    def swap_lane(g, s):
        return g ^ 1, s

    def shift(dr, df):
        return lambda g, s: (
            (g // LANES + dr) % counts[0] * LANES + g % LANES,
            (s // QUAD + df) % counts[1] * QUAD + s % QUAD,
        )

    held, inside = [None] * QUAD, [None] * QUAD
    held[ORDER[0]], inside[ORDER[0]] = first
    held[ORDER[0]] = moved(held[ORDER[0]], swap_quad(ORDER[0]))
    sent = slot_totals(ORDER[1:-1], reverse, *rest)
    rest = {**sent, **slot_totals(ORDER[-1:], reverse, *rest)}
    for o in ORDER[1:]:
        held[o], inside[o] = rest[o]
        if o:
            held[o] = moved(held[o], swap_quad(o))
    mine, rest = call(sum_kernel, [one, one], [*held], 1000, grant=2)
    near_shifts, far_shifts = range(1, counts[1]), far_shifts_of(counts)
    came_mine, came_other, came_both = [], [], []
    for df in near_shifts:
        came_mine.append(moved(mine, shift(0, df)))
    other = moved(rest, swap_lane)
    for df in near_shifts:
        came_other.append(moved(other, shift(0, df)))
    both = call(both_kernel, [one], [mine, other], 1000, grant=2)[0]
    for dr, df in far_shifts:
        came_both.append(moved(both, shift(dr, df)))
    kernel = functools.partial(base_kernel, near_shifts, far_shifts, counts, reverse)
    args = [mine, other, *came_mine, *came_other, *came_both]
    sum_mine, sum_other = call(kernel, [one, one], args, 1000, grant=2)
    other = moved(sum_other, swap_lane)
    kernel = functools.partial(back_sum_kernel, reverse)
    back = call(kernel, [two] * QUAD, [sum_mine, other, *held], 1000, grant=2)
    result = [back[0]] + [None] * (QUAD - 1)
    for o in ORDER[:-1]:
        result[o] = moved(back[o], swap_quad(o))
    return result, inside


def body(queries, key_rows, value_rows, norm_gain, cotangent):
    gain = norm_gain[None, :]
    first = first_totals(ORDER[0], key_rows, value_rows)
    keys, values, queries, cotangent = (near(a) for a in (key_rows, value_rows, queries, cotangent))
    carried, inside = carry(first, (keys, values), False)
    attended = local_part(queries, keys, values)
    scores = turned_scores(keys, queries)
    priors, sums = [None] * QUAD, []
    for o in EARLY:
        attended, *sums, priors[o] = attended_slot(
            o, carried[o], inside[o], attended, queries, cotangent, gain, sums
        )
    late = [o for o in ORDER if o not in EARLY]
    normed, grads, late_priors, first = norm(
        late, carried, inside, attended, queries, cotangent, gain, sums
    )
    for o, prior in zip(late, late_priors):
        priors[o] = prior
    carried, later = carry(first, (queries, grads), True)
    local_v, normed = value_part(scores, grads, normed)
    grad_q = query_part(grads, values, keys, priors)
    local_k, grad_q = turned_part(values, grads, queries, grad_q)
    args = local_k, local_v, keys, values, carried, later
    made = final_part((0,), *args)
    grad_k, grad_v = final_part(ORDER[:-1], *args, made)
    return normed, grad_q, grad_k, grad_v


def solution(mesh):
    rows = P(AXES, None)
    return jax.shard_map(
        body,
        mesh=mesh,
        in_specs=(rows, rows, rows, P(), rows),
        out_specs=(rows, rows, rows, rows),
        check_vma=False,
    )
```

```python
import functools

import jax
import jax.numpy as jnp
from jax import lax
from jax.experimental import pallas as pl
from jax.experimental.pallas import tpu as pltpu
from jax.sharding import PartitionSpec as P


H = 8
HD = 128
BLOCK = 512
EPSILON = 1e-06
AXES = ("grp", "seq")
LANES = 2
QUAD = 4
SHARE = H // (LANES * QUAD)
CUT = 256
SLAB = 512
ORDER = (3, 1, 2, 0)
EARLY = (0, 3)
UNROLL = 8
AHEAD = 2
PAIR = 2
F32 = jnp.float32
BF16 = jnp.bfloat16


def mm(a, b, ca, cb):
    return lax.dot_general(a, b, (((ca,), (cb,)), ((), ())), preferred_element_type=F32)


def vmem(*shape, dtype=F32):
    return pltpu.VMEM(shape, dtype)


def near(value):
    return pltpu.with_memory_space_constraint(value, pltpu.VMEM)


def far(value):
    return pltpu.with_memory_space_constraint(value, pltpu.HBM)


def place():
    grp, seq = lax.axis_index("grp"), lax.axis_index("seq")
    return lax.rem(grp, LANES), lax.rem(seq, QUAD), lax.div(grp, LANES), lax.div(seq, QUAD)


def call(kernel, out_shape, args, flops, scratch=(), grant=8, far_in=(), far_out=(), aliases=None):
    any_space = pl.BlockSpec(memory_space=pltpu.HBM)
    near_space = pl.BlockSpec(memory_space=pltpu.VMEM)
    return pl.pallas_call(
        lambda *refs: kernel(place(), *refs),
        out_shape=out_shape,
        in_specs=[any_space if i in far_in else near_space for i in range(len(args))],
        out_specs=[any_space if i in far_out else near_space for i in range(len(out_shape))],
        scratch_shapes=scratch,
        input_output_aliases=aliases or {},
        compiler_params=pltpu.CompilerParams(vmem_limit_bytes=grant << 20),
        cost_estimate=pl.CostEstimate(flops=flops, bytes_accessed=flops // 100, transcendentals=0),
    )(*[far(a) if i in far_in else near(a) for i, a in enumerate(args)])


def head_cols(head):
    return pl.ds(pl.multiple_of(head * HD, HD), HD)


def heads_of(slot, where):
    for lane in range(LANES):
        for share in range(SHARE):
            unit = (where[0] ^ lane) * QUAD + (where[1] ^ slot)
            yield lane, share, unit * SHARE + share


def slot_block(slot, reverse, where, block, blocks, a_ref, b_ref, piece_ref, inside_ref):
    rows = pl.ds(block * BLOCK, BLOCK)
    for lane, share, head in heads_of(slot, where):
        cols = head_cols(head)
        state = mm(a_ref[rows, cols], b_ref[rows, cols], 0, 0)
        if block == (blocks - 1 if reverse else 0):
            inside_ref[block, lane, share] = jnp.zeros_like(state)
            piece_ref[lane, share] = state
        else:
            run = piece_ref[lane, share]
            inside_ref[block, lane, share] = run
            piece_ref[lane, share] = run + state


def slot_kernel(slots, reverse, where, a_ref, b_ref, *outs):
    blocks = a_ref.shape[0] // BLOCK
    for i, slot in enumerate(slots):
        for block in reversed(range(blocks)) if reverse else range(blocks):
            slot_block(slot, reverse, where, block, blocks, a_ref, b_ref, *outs[2 * i : 2 * i + 2])


def slot_shapes(blocks):
    return [vmem(LANES, SHARE, HD, HD), vmem(blocks, LANES, SHARE, HD, HD)]


def slot_totals(slots, reverse, a, b):
    tokens, features = a.shape
    outs = call(
        functools.partial(slot_kernel, slots, reverse),
        slot_shapes(tokens // BLOCK) * len(slots),
        [a, b],
        2 * tokens * features // QUAD * len(slots) * HD,
    )
    return {slot: outs[2 * i : 2 * i + 2] for i, slot in enumerate(slots)}


def first_kernel(slot, where, k_far, v_far, piece_ref, inside_ref, k_ref, v_ref, sems):
    copies = []
    for at, (_, _, head) in enumerate(heads_of(slot, where)):
        for j, (source, target) in enumerate(((k_far, k_ref), (v_far, v_ref))):
            copy = pltpu.make_async_copy(source.at[:, head_cols(head)], target.at[at], sems.at[at, j])
            copy.start()
            copies.append(copy)
    for at, (lane, share, _) in enumerate(heads_of(slot, where)):
        copies[2 * at].wait()
        copies[2 * at + 1].wait()
        run = None
        for block in range(inside_ref.shape[0]):
            rows = pl.ds(block * BLOCK, BLOCK)
            state = mm(k_ref[at, rows, :], v_ref[at, rows, :], 0, 0)
            inside_ref[block, lane, share] = jnp.zeros_like(state) if run is None else run
            run = state if run is None else run + state
        piece_ref[lane, share] = run


def first_totals(slot, keys, values):
    tokens, _ = keys.shape
    heads = LANES * SHARE
    return call(
        functools.partial(first_kernel, slot),
        slot_shapes(tokens // BLOCK),
        [keys, values],
        2 * tokens * heads * HD * HD,
        scratch=[vmem(heads, tokens, HD, dtype=BF16)] * 2 + [pltpu.SemaphoreType.DMA((heads, 2))],
        far_in=(0, 1),
    )


def triangle(size, upper=False):
    row = lax.broadcasted_iota(jnp.int32, (size, size), 0)
    col = lax.broadcasted_iota(jnp.int32, (size, size), 1)
    return row <= col if upper else row >= col


def over_units(blocks, step, first=0, heads=H, most=UNROLL):
    count = blocks * heads
    unroll = max(u for u in range(1, most + 1) if count % u == 0)

    def several(i, _):
        for j in range(unroll):
            unit = i * unroll + j
            step(unit // heads, first + unit % heads)
        return 0

    lax.fori_loop(0, count // unroll, several, 0)


def block_part(block, first, count):
    return pl.ds(pl.multiple_of(block * BLOCK + first * CUT, CUT), count * CUT)


def attend(block, cols, a_ref, b_ref, c_ref, mask, turned):
    tiles = BLOCK // CUT
    sums = [None] * tiles
    for j in range(tiles):
        first, count = (0, j + 1) if turned else (j, tiles - j)
        rows, here = block_part(block, first, count), block_part(block, j, 1)
        scores = mm(a_ref[rows, cols], b_ref[here, cols], 1, 1)
        at = (j - first) * CUT
        parts = [jnp.where(mask, scores[at : at + CUT], 0.0)]
        if at:
            parts.insert(0, scores[:at])
        if at + CUT < count * CUT:
            parts.append(scores[at + CUT :])
        scores = jnp.concatenate([part.astype(BF16) for part in parts], axis=0)
        product = mm(scores, c_ref[here, cols], 1, 0)
        for i in range(count):
            value = product[i * CUT : (i + 1) * CUT]
            sums[first + i] = value if sums[first + i] is None else sums[first + i] + value
    return sums


def local_kernel(where, q_ref, k_ref, v_ref, out_ref):
    mask = triangle(CUT)

    def step(block, head):
        cols = head_cols(head)
        sums = attend(block, cols, q_ref, k_ref, v_ref, mask, False)
        for i, value in enumerate(sums):
            out_ref[block_part(block, i, 1), cols] = value

    over_units(q_ref.shape[0] // BLOCK, step, most=4)


def local_part(queries, keys, values):
    tokens, features = queries.shape
    return call(
        local_kernel,
        [vmem(tokens, features)],
        [queries, keys, values],
        4 * tokens * BLOCK * features,
    )[0]


def scores_kernel(where, k_ref, q_ref, out_ref):
    mask = triangle(CUT, True)

    def step(block, head):
        cols = head_cols(head)
        for j in range(BLOCK // CUT):
            rows, here = block_part(block, 0, j + 1), block_part(block, j, 1)
            scores = mm(k_ref[rows, cols], q_ref[here, cols], 1, 1)
            to = pl.ds(j * CUT, CUT)
            out_ref[block, head, to, to] = jnp.where(mask, scores[j * CUT :], 0.0).astype(BF16)
            if j:
                out_ref[block, head, pl.ds(0, j * CUT), to] = scores[: j * CUT].astype(BF16)

    over_units(k_ref.shape[0] // BLOCK, step, most=4)


def turned_scores(keys, queries):
    tokens, features = keys.shape
    return call(
        scores_kernel,
        [vmem(tokens // BLOCK, H, BLOCK, BLOCK, dtype=BF16)],
        [keys, queries],
        2 * tokens * BLOCK * features,
    )[0]


def value_kernel(where, scores_ref, g_ref, ready_ref, out_ref, far_ref, sem):
    copy = pltpu.make_async_copy(ready_ref, far_ref, sem)
    copy.start()

    def step(block, head):
        cols = head_cols(head)
        tiles = BLOCK // CUT
        sums = [None] * tiles
        for j in range(tiles):
            rows = pl.ds(0, (j + 1) * CUT)
            scores = scores_ref[block, head, rows, pl.ds(j * CUT, CUT)]
            product = mm(scores, g_ref[block_part(block, j, 1), cols], 1, 0)
            for i in range(j + 1):
                value = product[i * CUT : (i + 1) * CUT]
                sums[i] = value if sums[i] is None else sums[i] + value
        for i, value in enumerate(sums):
            out_ref[block_part(block, i, 1), cols] = value

    over_units(g_ref.shape[0] // BLOCK, step)
    copy.wait()


def value_part(scores, grads, ready):
    tokens, features = grads.shape
    return call(
        value_kernel,
        [vmem(tokens, features), jax.ShapeDtypeStruct(ready.shape, ready.dtype)],
        [scores, grads, ready],
        2 * tokens * BLOCK * features,
        scratch=[pltpu.SemaphoreType.DMA(())],
        far_out=(1,),
    )


def attended_kernel(slot, first, where, carried_ref, inside_ref, local_ref, q_ref, dy_ref, gain_ref, *refs):
    if first:
        att_ref, square_ref, cross_ref, prior_ref = refs
    else:
        old_square, old_cross, att_ref, square_ref, cross_ref, prior_ref = refs
    blocks = q_ref.shape[0] // BLOCK
    for block in range(blocks):
        rows = pl.ds(block * BLOCK, BLOCK)
        square = None if first else old_square[rows, :]
        cross = None if first else old_cross[rows, :]
        for lane, share, head in heads_of(slot, where):
            cols = head_cols(head)
            prior = (carried_ref[lane, share] + inside_ref[block, lane, share]).astype(BF16)
            prior_ref[block, lane, share] = prior
            att = local_ref[rows, cols] + mm(q_ref[rows, cols], prior, 1, 0)
            att_ref[rows, cols] = att
            term = dy_ref[rows, cols].astype(F32) * gain_ref[:, cols] * att
            square = att * att if square is None else square + att * att
            cross = term if cross is None else cross + term
        square_ref[rows, :] = square
        cross_ref[rows, :] = cross


def attended_slot(slot, carried, inside, local, queries, cotangent, gain, sums):
    tokens, features = queries.shape
    blocks = tokens // BLOCK
    first = not sums
    return call(
        functools.partial(attended_kernel, slot, first),
        [vmem(tokens, features), vmem(tokens, HD), vmem(tokens, HD)]
        + [vmem(blocks, LANES, SHARE, HD, HD, dtype=BF16)],
        [carried, inside, local, queries, cotangent, gain, *sums],
        2 * tokens * features // QUAD * HD,
        aliases={2: 0},
    )


def norm_kernel(slots, where, *refs):
    count = len(slots)
    carried, inside = refs[:count], refs[count : 2 * count]
    local_ref, q_ref, dy_ref, gain_ref, old_square, old_cross = refs[2 * count : 2 * count + 6]
    outs = refs[2 * count + 6 :]
    att_ref, out_ref, grad_ref = outs[:3]
    priors, (piece_ref, later_ref, square_ref, cross_ref) = outs[3 : 3 + count], outs[3 + count :]
    blocks = q_ref.shape[0] // BLOCK
    features = H * HD
    for block in reversed(range(blocks)):
        rows = pl.ds(block * BLOCK, BLOCK)
        square, cross = old_square[rows, :], old_cross[rows, :]
        for i, slot in enumerate(slots):
            for lane, share, head in heads_of(slot, where):
                cols = head_cols(head)
                prior = (carried[i][lane, share] + inside[i][block, lane, share]).astype(BF16)
                priors[i][block, lane, share] = prior
                att = local_ref[rows, cols] + mm(q_ref[rows, cols], prior, 1, 0)
                att_ref[rows, cols] = att
                square += att * att
                cross += dy_ref[rows, cols].astype(F32) * gain_ref[:, cols] * att
        square_ref[...], cross_ref[...] = square, cross

        def step(i, _):
            here = pl.ds(pl.multiple_of(i * SLAB, SLAB), SLAB)
            rows = pl.ds(pl.multiple_of(block * BLOCK + i * SLAB, SLAB), SLAB)
            square = jnp.sum(square_ref[here, :], axis=1, keepdims=True) / features
            inverse = lax.rsqrt(square + EPSILON)
            mean = inverse * (jnp.sum(cross_ref[here, :], axis=1, keepdims=True) / features)
            weight = inverse * inverse * mean
            inverse, weight = (jnp.broadcast_to(x, (SLAB, HD)) for x in (inverse, weight))
            for head in range(H):
                cols = pl.ds(head * HD, HD)
                att = att_ref[rows, cols]
                gain = gain_ref[:, cols] * inverse
                out_ref[rows, cols] = (att * gain).astype(BF16)
                scaled = dy_ref[rows, cols].astype(F32) * gain
                grad_ref[rows, cols] = (scaled - att * weight).astype(BF16)
            return 0

        lax.fori_loop(0, BLOCK // SLAB, step, 0)
        slot_block(ORDER[0], True, where, block, blocks, q_ref, grad_ref, piece_ref, later_ref)


def norm(slots, carried, inside, attended, queries, cotangent, gain, sums):
    tokens, features = attended.shape
    blocks = tokens // BLOCK
    half = vmem(tokens, features, dtype=BF16)
    prior = vmem(blocks, LANES, SHARE, HD, HD, dtype=BF16)
    carried, inside = [carried[o] for o in slots], [inside[o] for o in slots]
    _, normed, grads, *outs = call(
        functools.partial(norm_kernel, slots),
        [vmem(tokens, features), half, half] + [prior] * len(slots) + slot_shapes(blocks),
        [*carried, *inside, attended, queries, cotangent, gain, *sums],
        20 * tokens * features,
        scratch=[vmem(BLOCK, HD)] * 2,
        aliases={2 * len(slots): 0},
    )
    return normed, grads, outs[: len(slots)], outs[len(slots) :]


def query_kernel(where, g_ref, v_ref, k_ref, *refs):
    priors, (out_ref, prior_ref) = refs[:QUAD], refs[QUAD:]
    mask = triangle(CUT)
    prior_ref[...] = jnp.zeros_like(prior_ref)
    for slot in range(QUAD):
        for lane, share, head in heads_of(slot, where):
            cols = head_cols(head % PAIR)
            for block in range(prior_ref.shape[0]):
                prior_ref[block, head // PAIR, cols, cols] = priors[slot][block, lane, share]

    def step(block, pair):
        wide = pl.ds(pl.multiple_of(pair * PAIR * HD, PAIR * HD), PAIR * HD)
        rows = block_part(block, 0, BLOCK // CUT)
        far_part = mm(g_ref[rows, wide], prior_ref[block, pair], 1, 1)
        for j in range(PAIR):
            cols = head_cols(pair * PAIR + j)
            sums = attend(block, cols, g_ref, v_ref, k_ref, mask, False)
            for i, value in enumerate(sums):
                value += far_part[i * CUT : (i + 1) * CUT, j * HD : (j + 1) * HD]
                out_ref[block_part(block, i, 1), cols] = value.astype(BF16)

    def several(i, _):
        for j in range(UNROLL // PAIR):
            unit = i * (UNROLL // PAIR) + j
            step(unit // (H // PAIR), unit % (H // PAIR))
        return 0

    lax.fori_loop(0, g_ref.shape[0] // BLOCK * H // UNROLL, several, 0)


def query_part(grads, values, keys, priors):
    tokens, features = grads.shape
    return call(
        query_kernel,
        [vmem(tokens, features, dtype=BF16)],
        [grads, values, keys, *priors],
        4 * tokens * BLOCK * features,
        scratch=[vmem(tokens // BLOCK, H // PAIR, PAIR * HD, PAIR * HD, dtype=BF16)],
    )[0]


def turned_kernel(first, heads, ready, where, a_ref, b_ref, c_ref, *refs):
    if ready:
        ready_ref, out_ref, far_ref, sem = refs[-4:]
        copy = pltpu.make_async_copy(ready_ref, far_ref, sem)
        copy.start()
    else:
        out_ref = refs[-1]
    mask = triangle(CUT, True)

    def step(block, head):
        cols = head_cols(head)
        sums = attend(block, cols, a_ref, b_ref, c_ref, mask, True)
        for i, value in enumerate(sums):
            out_ref[block_part(block, i, 1), cols] = value

    over_units(a_ref.shape[0] // BLOCK, step, first, heads)
    if ready:
        copy.wait()


def turned_part(first, heads, a, b, c, made=(), ready=()):
    tokens, features = a.shape
    return call(
        functools.partial(turned_kernel, first, heads, len(ready)),
        [vmem(tokens, features)] + [jax.ShapeDtypeStruct(r.shape, r.dtype) for r in ready],
        [a, b, c, *made, *ready],
        4 * tokens * BLOCK * heads * HD,
        scratch=[pltpu.SemaphoreType.DMA(())] * len(ready),
        far_out=(1,) if ready else (),
        aliases={3: 0} if made else None,
    )


def final_kernel(slots, where, lk_ref, lv_ref, k_ref, v_ref, *refs):
    count = len(slots)
    carried, later = refs[:count], refs[count : 2 * count]
    gk_far, gv_far, gk_ref, gv_ref, sems = refs[-5:]
    copies = []
    for i, slot in enumerate(slots):
        for lane, share, head in heads_of(slot, where):
            cols, at = head_cols(head), len(copies) // 2
            for block in range(k_ref.shape[0] // BLOCK):
                rows = pl.ds(block * BLOCK, BLOCK)
                state = (carried[i][lane, share] + later[i][block, lane, share]).astype(BF16)
                grad_k = lk_ref[rows, cols] + mm(v_ref[rows, cols], state, 1, 1)
                grad_v = lv_ref[rows, cols] + mm(k_ref[rows, cols], state, 1, 0)
                gk_ref[at, rows, :], gv_ref[at, rows, :] = grad_k.astype(BF16), grad_v.astype(BF16)
            for j, (source, target) in enumerate(((gk_ref, gk_far), (gv_ref, gv_far))):
                copy = pltpu.make_async_copy(source.at[at], target.at[:, cols], sems.at[at, j])
                copy.start()
                copies.append(copy)
    for copy in copies:
        copy.wait()


def final_part(slots, local_k, local_v, keys, values, carried, later, made=()):
    tokens, features = keys.shape
    heads = len(slots) * LANES * SHARE
    args = [local_k, local_v, keys, values]
    args += [carried[o] for o in slots] + [later[o] for o in slots]
    places = range(len(args), len(args) + len(made))
    return call(
        functools.partial(final_kernel, slots),
        [jax.ShapeDtypeStruct((tokens, features), BF16)] * 2,
        [*args, *made],
        4 * tokens * heads * HD * HD,
        scratch=[vmem(heads, tokens, HD, dtype=BF16)] * 2 + [pltpu.SemaphoreType.DMA((heads, 2))],
        far_in=places,
        far_out=(0, 1),
        grant=12,
        aliases={place: i for i, place in enumerate(places)},
    )


def moved(value, move):
    groups, shards = lax.axis_size("grp"), lax.axis_size("seq")
    pairs = []
    for g in range(groups):
        for s in range(shards):
            to_g, to_s = move(g, s)
            pairs.append((g * shards + s, to_g * shards + to_s))
    return lax.ppermute(value, AXES, pairs)


def sum_kernel(where, *refs):
    held, (mine_ref, rest_ref) = refs[:QUAD], refs[QUAD:]
    for lane, out in enumerate((mine_ref, rest_ref)):
        out[...] = (held[0][lane] + held[1][lane]) + (held[2][lane] + held[3][lane])


def both_kernel(where, mine_ref, other_ref, both_ref):
    both_ref[...] = mine_ref[...] + other_ref[...]


def before(a, b, reverse):
    return a > b if reverse else a < b


def base_kernel(near_shifts, far_shifts, counts, reverse, where, mine_ref, other_ref, *refs):
    refs = list(refs)
    lane, row, far_row = where[0], where[2], where[3]
    takes = lane == (0 if reverse else 1)
    sum_mine = jnp.where(takes, other_ref[...], 0.0)
    sum_other = jnp.where(takes, 0.0, mine_ref[...])
    near_mine = [refs.pop(0) for _ in near_shifts]
    near_other = [refs.pop(0) for _ in near_shifts]
    for df, mine, other in zip(near_shifts, near_mine, near_other):
        near_by = before(lax.rem(far_row - df + counts[1], counts[1]), far_row, reverse)
        mine, other = mine[...], other[...]
        sum_mine += jnp.where(near_by, mine, 0.0) + jnp.where(takes, other, 0.0)
        sum_other += jnp.where(near_by, other, 0.0) + jnp.where(takes, 0.0, mine)
    for dr, _ in far_shifts:
        source = lax.rem(row - dr + counts[0], counts[0])
        add = jnp.where(before(source, row, reverse), refs.pop(0)[...], 0.0)
        sum_mine, sum_other = sum_mine + add, sum_other + add
    refs[0][...], refs[1][...] = sum_mine, sum_other


def back_sum_kernel(reverse, where, mine_ref, other_ref, *refs):
    held, back = refs[:QUAD], refs[QUAD:]
    quad = where[1]
    for lane, base in enumerate((mine_ref, other_ref)):
        for o in range(QUAD):
            value = base[...]
            for i in range(QUAD):
                if i != o:
                    near_by = before(quad ^ i, quad ^ o, reverse)
                    value += jnp.where(near_by, held[i][lane], 0.0)
            back[o][lane] = value


def far_shifts_of(counts):
    shifts = [(dr, df) for dr in range(1, counts[0]) for df in range(counts[1])]
    return sorted(shifts, key=lambda shift: -sum(shift))


def carry(first, rest, reverse):
    counts = lax.axis_size("grp") // LANES, lax.axis_size("seq") // QUAD
    one, two = vmem(SHARE, HD, HD), vmem(LANES, SHARE, HD, HD)

    def swap_quad(o):
        return lambda g, s: (g, s ^ o)

    def swap_lane(g, s):
        return g ^ 1, s

    def shift(dr, df):
        return lambda g, s: (
            (g // LANES + dr) % counts[0] * LANES + g % LANES,
            (s // QUAD + df) % counts[1] * QUAD + s % QUAD,
        )

    held, inside = [None] * QUAD, [None] * QUAD
    held[ORDER[0]], inside[ORDER[0]] = first
    held[ORDER[0]] = moved(held[ORDER[0]], swap_quad(ORDER[0]))
    sent = slot_totals(ORDER[1:-1], reverse, *rest)
    rest = {**sent, **slot_totals(ORDER[-1:], reverse, *rest)}
    for o in ORDER[1:]:
        held[o], inside[o] = rest[o]
        if o:
            held[o] = moved(held[o], swap_quad(o))
    mine, rest = call(sum_kernel, [one, one], [*held], 1000, grant=2)
    near_shifts, far_shifts = range(1, counts[1]), far_shifts_of(counts)
    came_mine, came_other, came_both = [], [], []
    for df in near_shifts:
        came_mine.append(moved(mine, shift(0, df)))
    other = moved(rest, swap_lane)
    for df in near_shifts:
        came_other.append(moved(other, shift(0, df)))
    both = call(both_kernel, [one], [mine, other], 1000, grant=2)[0]
    for dr, df in far_shifts:
        came_both.append(moved(both, shift(dr, df)))
    kernel = functools.partial(base_kernel, near_shifts, far_shifts, counts, reverse)
    args = [mine, other, *came_mine, *came_other, *came_both]
    sum_mine, sum_other = call(kernel, [one, one], args, 1000, grant=2)
    other = moved(sum_other, swap_lane)
    kernel = functools.partial(back_sum_kernel, reverse)
    back = call(kernel, [two] * QUAD, [sum_mine, other, *held], 1000, grant=2)
    result = [back[0]] + [None] * (QUAD - 1)
    for o in ORDER[:-1]:
        result[o] = moved(back[o], swap_quad(o))
    return result, inside


def body(queries, key_rows, value_rows, norm_gain, cotangent):
    gain = norm_gain[None, :]
    first = first_totals(ORDER[0], key_rows, value_rows)
    keys, values, queries, cotangent = (near(a) for a in (key_rows, value_rows, queries, cotangent))
    carried, inside = carry(first, (keys, values), False)
    attended = local_part(queries, keys, values)
    scores = turned_scores(keys, queries)
    priors, sums = [None] * QUAD, []
    for o in EARLY:
        attended, *sums, priors[o] = attended_slot(
            o, carried[o], inside[o], attended, queries, cotangent, gain, sums
        )
    late = [o for o in ORDER if o not in EARLY]
    normed, grads, late_priors, first = norm(
        late, carried, inside, attended, queries, cotangent, gain, sums
    )
    for o, prior in zip(late, late_priors):
        priors[o] = prior
    carried, later = carry(first, (queries, grads), True)
    local_v, normed = value_part(scores, grads, normed)
    local_k = turned_part(0, AHEAD, values, grads, queries)
    grad_q = query_part(grads, values, keys, priors)
    local_k, grad_q = turned_part(AHEAD, H - AHEAD, values, grads, queries, local_k, [grad_q])
    args = local_k, local_v, keys, values, carried, later
    made = final_part((0,) + ORDER[:1], *args)
    grad_k, grad_v = final_part(ORDER[1:-1], *args, made)
    return normed, grad_q, grad_k, grad_v


def solution(mesh):
    rows = P(AXES, None)
    return jax.shard_map(
        body,
        mesh=mesh,
        in_specs=(rows, rows, rows, P(), rows),
        out_specs=(rows, rows, rows, rows),
        check_vma=False,
    )
```

```python
import functools

import jax
import jax.numpy as jnp
from jax import lax
from jax.experimental import pallas as pl
from jax.experimental.pallas import tpu as pltpu
from jax.sharding import PartitionSpec as P


H = 8
HD = 128
BLOCK = 512
EPSILON = 1e-06
AXES = ("grp", "seq")
LANES = 2
QUAD = 4
SHARE = H // (LANES * QUAD)
CUT = 256
SLAB = 512
ORDER = (3, 1, 2, 0)
EARLY = (0, 3)
UNROLL = 8
AHEAD = 2
PAIR = 2
F32 = jnp.float32
BF16 = jnp.bfloat16


def mm(a, b, ca, cb):
    return lax.dot_general(a, b, (((ca,), (cb,)), ((), ())), preferred_element_type=F32)


def vmem(*shape, dtype=F32):
    return pltpu.VMEM(shape, dtype)


def near(value):
    return pltpu.with_memory_space_constraint(value, pltpu.VMEM)


def far(value):
    return pltpu.with_memory_space_constraint(value, pltpu.HBM)


def place():
    grp, seq = lax.axis_index("grp"), lax.axis_index("seq")
    return lax.rem(grp, LANES), lax.rem(seq, QUAD), lax.div(grp, LANES), lax.div(seq, QUAD)


def call(kernel, out_shape, args, flops, scratch=(), grant=8, far_in=(), far_out=(), aliases=None):
    any_space = pl.BlockSpec(memory_space=pltpu.HBM)
    near_space = pl.BlockSpec(memory_space=pltpu.VMEM)
    return pl.pallas_call(
        lambda *refs: kernel(place(), *refs),
        out_shape=out_shape,
        in_specs=[any_space if i in far_in else near_space for i in range(len(args))],
        out_specs=[any_space if i in far_out else near_space for i in range(len(out_shape))],
        scratch_shapes=scratch,
        input_output_aliases=aliases or {},
        compiler_params=pltpu.CompilerParams(vmem_limit_bytes=grant << 20),
        cost_estimate=pl.CostEstimate(flops=flops, bytes_accessed=flops // 100, transcendentals=0),
    )(*[far(a) if i in far_in else near(a) for i, a in enumerate(args)])


def head_cols(head):
    return pl.ds(pl.multiple_of(head * HD, HD), HD)


def heads_of(slot, where):
    for lane in range(LANES):
        for share in range(SHARE):
            unit = (where[0] ^ lane) * QUAD + (where[1] ^ slot)
            yield lane, share, unit * SHARE + share


def slot_block(slot, reverse, where, block, blocks, a_ref, b_ref, piece_ref, inside_ref):
    rows = pl.ds(block * BLOCK, BLOCK)
    for lane, share, head in heads_of(slot, where):
        cols = head_cols(head)
        state = mm(a_ref[rows, cols], b_ref[rows, cols], 0, 0)
        if block == (blocks - 1 if reverse else 0):
            inside_ref[block, lane, share] = jnp.zeros_like(state)
            piece_ref[lane, share] = state
        else:
            run = piece_ref[lane, share]
            inside_ref[block, lane, share] = run
            piece_ref[lane, share] = run + state


def slot_kernel(slots, reverse, where, a_ref, b_ref, *outs):
    blocks = a_ref.shape[0] // BLOCK
    for i, slot in enumerate(slots):
        for block in reversed(range(blocks)) if reverse else range(blocks):
            slot_block(slot, reverse, where, block, blocks, a_ref, b_ref, *outs[2 * i : 2 * i + 2])


def slot_shapes(blocks):
    return [vmem(LANES, SHARE, HD, HD), vmem(blocks, LANES, SHARE, HD, HD)]


def slot_totals(slots, reverse, a, b):
    tokens, features = a.shape
    outs = call(
        functools.partial(slot_kernel, slots, reverse),
        slot_shapes(tokens // BLOCK) * len(slots),
        [a, b],
        2 * tokens * features // QUAD * len(slots) * HD,
    )
    return {slot: outs[2 * i : 2 * i + 2] for i, slot in enumerate(slots)}


def first_kernel(slot, where, k_far, v_far, piece_ref, inside_ref, k_ref, v_ref, sems):
    copies = []
    for at, (_, _, head) in enumerate(heads_of(slot, where)):
        for j, (source, target) in enumerate(((k_far, k_ref), (v_far, v_ref))):
            copy = pltpu.make_async_copy(source.at[:, head_cols(head)], target.at[at], sems.at[at, j])
            copy.start()
            copies.append(copy)
    for at, (lane, share, _) in enumerate(heads_of(slot, where)):
        copies[2 * at].wait()
        copies[2 * at + 1].wait()
        run = None
        for block in range(inside_ref.shape[0]):
            rows = pl.ds(block * BLOCK, BLOCK)
            state = mm(k_ref[at, rows, :], v_ref[at, rows, :], 0, 0)
            inside_ref[block, lane, share] = jnp.zeros_like(state) if run is None else run
            run = state if run is None else run + state
        piece_ref[lane, share] = run


def first_totals(slot, keys, values):
    tokens, _ = keys.shape
    heads = LANES * SHARE
    return call(
        functools.partial(first_kernel, slot),
        slot_shapes(tokens // BLOCK),
        [keys, values],
        2 * tokens * heads * HD * HD,
        scratch=[vmem(heads, tokens, HD, dtype=BF16)] * 2 + [pltpu.SemaphoreType.DMA((heads, 2))],
        far_in=(0, 1),
    )


def triangle(size, upper=False):
    row = lax.broadcasted_iota(jnp.int32, (size, size), 0)
    col = lax.broadcasted_iota(jnp.int32, (size, size), 1)
    return row <= col if upper else row >= col


def over_units(blocks, step, first=0, heads=H, most=UNROLL):
    count = blocks * heads
    unroll = max(u for u in range(1, most + 1) if count % u == 0)

    def several(i, _):
        for j in range(unroll):
            unit = i * unroll + j
            step(unit // heads, first + unit % heads)
        return 0

    lax.fori_loop(0, count // unroll, several, 0)


def block_part(block, first, count):
    return pl.ds(pl.multiple_of(block * BLOCK + first * CUT, CUT), count * CUT)


def attend(block, cols, a_ref, b_ref, c_ref, mask, turned):
    tiles = BLOCK // CUT
    sums = [None] * tiles
    for j in range(tiles):
        first, count = (0, j + 1) if turned else (j, tiles - j)
        rows, here = block_part(block, first, count), block_part(block, j, 1)
        scores = mm(a_ref[rows, cols], b_ref[here, cols], 1, 1)
        at = (j - first) * CUT
        parts = [jnp.where(mask, scores[at : at + CUT], 0.0)]
        if at:
            parts.insert(0, scores[:at])
        if at + CUT < count * CUT:
            parts.append(scores[at + CUT :])
        scores = jnp.concatenate([part.astype(BF16) for part in parts], axis=0)
        product = mm(scores, c_ref[here, cols], 1, 0)
        for i in range(count):
            value = product[i * CUT : (i + 1) * CUT]
            sums[first + i] = value if sums[first + i] is None else sums[first + i] + value
    return sums


def local_kernel(where, q_ref, k_ref, v_ref, out_ref):
    mask = triangle(CUT)

    def step(block, head):
        cols = head_cols(head)
        sums = attend(block, cols, q_ref, k_ref, v_ref, mask, False)
        for i, value in enumerate(sums):
            out_ref[block_part(block, i, 1), cols] = value

    over_units(q_ref.shape[0] // BLOCK, step, most=4)


def local_part(queries, keys, values):
    tokens, features = queries.shape
    return call(
        local_kernel,
        [vmem(tokens, features)],
        [queries, keys, values],
        4 * tokens * BLOCK * features,
    )[0]


def scores_kernel(where, k_ref, q_ref, out_ref):
    mask = triangle(CUT, True)

    def step(block, head):
        cols = head_cols(head)
        for j in range(BLOCK // CUT):
            rows, here = block_part(block, 0, j + 1), block_part(block, j, 1)
            scores = mm(k_ref[rows, cols], q_ref[here, cols], 1, 1)
            to = pl.ds(j * CUT, CUT)
            out_ref[block, head, to, to] = jnp.where(mask, scores[j * CUT :], 0.0).astype(BF16)
            if j:
                out_ref[block, head, pl.ds(0, j * CUT), to] = scores[: j * CUT].astype(BF16)

    over_units(k_ref.shape[0] // BLOCK, step, most=4)


def turned_scores(keys, queries):
    tokens, features = keys.shape
    return call(
        scores_kernel,
        [vmem(tokens // BLOCK, H, BLOCK, BLOCK, dtype=BF16)],
        [keys, queries],
        2 * tokens * BLOCK * features,
    )[0]


def value_kernel(where, scores_ref, g_ref, ready_ref, out_ref, far_ref, sem):
    copy = pltpu.make_async_copy(ready_ref, far_ref, sem)
    copy.start()

    def step(block, head):
        cols = head_cols(head)
        tiles = BLOCK // CUT
        sums = [None] * tiles
        for j in range(tiles):
            rows = pl.ds(0, (j + 1) * CUT)
            scores = scores_ref[block, head, rows, pl.ds(j * CUT, CUT)]
            product = mm(scores, g_ref[block_part(block, j, 1), cols], 1, 0)
            for i in range(j + 1):
                value = product[i * CUT : (i + 1) * CUT]
                sums[i] = value if sums[i] is None else sums[i] + value
        for i, value in enumerate(sums):
            out_ref[block_part(block, i, 1), cols] = value

    over_units(g_ref.shape[0] // BLOCK, step)
    copy.wait()


def value_part(scores, grads, ready):
    tokens, features = grads.shape
    return call(
        value_kernel,
        [vmem(tokens, features), jax.ShapeDtypeStruct(ready.shape, ready.dtype)],
        [scores, grads, ready],
        2 * tokens * BLOCK * features,
        scratch=[pltpu.SemaphoreType.DMA(())],
        far_out=(1,),
    )


def attended_kernel(slot, first, where, carried_ref, inside_ref, local_ref, q_ref, dy_ref, gain_ref, *refs):
    if first:
        att_ref, square_ref, cross_ref, prior_ref = refs
    else:
        old_square, old_cross, att_ref, square_ref, cross_ref, prior_ref = refs
    blocks = q_ref.shape[0] // BLOCK
    for block in range(blocks):
        rows = pl.ds(block * BLOCK, BLOCK)
        square = None if first else old_square[rows, :]
        cross = None if first else old_cross[rows, :]
        for lane, share, head in heads_of(slot, where):
            cols = head_cols(head)
            prior = (carried_ref[lane, share] + inside_ref[block, lane, share]).astype(BF16)
            prior_ref[block, lane, share] = prior
            att = local_ref[rows, cols] + mm(q_ref[rows, cols], prior, 1, 0)
            att_ref[rows, cols] = att
            term = dy_ref[rows, cols].astype(F32) * gain_ref[:, cols] * att
            square = att * att if square is None else square + att * att
            cross = term if cross is None else cross + term
        square_ref[rows, :] = square
        cross_ref[rows, :] = cross


def attended_slot(slot, carried, inside, local, queries, cotangent, gain, sums):
    tokens, features = queries.shape
    blocks = tokens // BLOCK
    first = not sums
    return call(
        functools.partial(attended_kernel, slot, first),
        [vmem(tokens, features), vmem(tokens, HD), vmem(tokens, HD)]
        + [vmem(blocks, LANES, SHARE, HD, HD, dtype=BF16)],
        [carried, inside, local, queries, cotangent, gain, *sums],
        2 * tokens * features // QUAD * HD,
        aliases={2: 0},
    )


def norm_kernel(slots, where, *refs):
    count = len(slots)
    carried, inside = refs[:count], refs[count : 2 * count]
    local_ref, q_ref, dy_ref, gain_ref, old_square, old_cross = refs[2 * count : 2 * count + 6]
    outs = refs[2 * count + 6 :]
    att_ref, out_ref, grad_ref = outs[:3]
    priors, (piece_ref, later_ref, square_ref, cross_ref) = outs[3 : 3 + count], outs[3 + count :]
    blocks = q_ref.shape[0] // BLOCK
    features = H * HD
    for block in reversed(range(blocks)):
        rows = pl.ds(block * BLOCK, BLOCK)
        square, cross = old_square[rows, :], old_cross[rows, :]
        for i, slot in enumerate(slots):
            for lane, share, head in heads_of(slot, where):
                cols = head_cols(head)
                prior = (carried[i][lane, share] + inside[i][block, lane, share]).astype(BF16)
                priors[i][block, lane, share] = prior
                att = local_ref[rows, cols] + mm(q_ref[rows, cols], prior, 1, 0)
                att_ref[rows, cols] = att
                square += att * att
                cross += dy_ref[rows, cols].astype(F32) * gain_ref[:, cols] * att
        square_ref[...], cross_ref[...] = square, cross

        def step(i, _):
            here = pl.ds(pl.multiple_of(i * SLAB, SLAB), SLAB)
            rows = pl.ds(pl.multiple_of(block * BLOCK + i * SLAB, SLAB), SLAB)
            square = jnp.sum(square_ref[here, :], axis=1, keepdims=True) / features
            inverse = lax.rsqrt(square + EPSILON)
            mean = inverse * (jnp.sum(cross_ref[here, :], axis=1, keepdims=True) / features)
            weight = inverse * inverse * mean
            inverse, weight = (jnp.broadcast_to(x, (SLAB, HD)) for x in (inverse, weight))
            for head in range(H):
                cols = pl.ds(head * HD, HD)
                att = att_ref[rows, cols]
                gain = gain_ref[:, cols] * inverse
                out_ref[rows, cols] = (att * gain).astype(BF16)
                scaled = dy_ref[rows, cols].astype(F32) * gain
                grad_ref[rows, cols] = (scaled - att * weight).astype(BF16)
            return 0

        lax.fori_loop(0, BLOCK // SLAB, step, 0)
        slot_block(ORDER[0], True, where, block, blocks, q_ref, grad_ref, piece_ref, later_ref)


def norm(slots, carried, inside, attended, queries, cotangent, gain, sums):
    tokens, features = attended.shape
    blocks = tokens // BLOCK
    half = vmem(tokens, features, dtype=BF16)
    prior = vmem(blocks, LANES, SHARE, HD, HD, dtype=BF16)
    carried, inside = [carried[o] for o in slots], [inside[o] for o in slots]
    _, normed, grads, *outs = call(
        functools.partial(norm_kernel, slots),
        [vmem(tokens, features), half, half] + [prior] * len(slots) + slot_shapes(blocks),
        [*carried, *inside, attended, queries, cotangent, gain, *sums],
        20 * tokens * features,
        scratch=[vmem(BLOCK, HD)] * 2,
        aliases={2 * len(slots): 0},
    )
    return normed, grads, outs[: len(slots)], outs[len(slots) :]


def query_kernel(where, g_ref, v_ref, k_ref, *refs):
    priors, (out_ref, prior_ref) = refs[:QUAD], refs[QUAD:]
    mask = triangle(CUT)
    prior_ref[...] = jnp.zeros_like(prior_ref)
    for slot in range(QUAD):
        for lane, share, head in heads_of(slot, where):
            cols = head_cols(head % PAIR)
            for block in range(prior_ref.shape[0]):
                prior_ref[block, head // PAIR, cols, cols] = priors[slot][block, lane, share]

    def step(block, pair):
        wide = pl.ds(pl.multiple_of(pair * PAIR * HD, PAIR * HD), PAIR * HD)
        rows = block_part(block, 0, BLOCK // CUT)
        far_part = mm(g_ref[rows, wide], prior_ref[block, pair], 1, 1)
        for j in range(PAIR):
            cols = head_cols(pair * PAIR + j)
            sums = attend(block, cols, g_ref, v_ref, k_ref, mask, False)
            for i, value in enumerate(sums):
                value += far_part[i * CUT : (i + 1) * CUT, j * HD : (j + 1) * HD]
                out_ref[block_part(block, i, 1), cols] = value.astype(BF16)

    def several(i, _):
        for j in range(UNROLL // PAIR):
            unit = i * (UNROLL // PAIR) + j
            step(unit // (H // PAIR), unit % (H // PAIR))
        return 0

    lax.fori_loop(0, g_ref.shape[0] // BLOCK * H // UNROLL, several, 0)


def query_part(grads, values, keys, priors):
    tokens, features = grads.shape
    return call(
        query_kernel,
        [vmem(tokens, features, dtype=BF16)],
        [grads, values, keys, *priors],
        4 * tokens * BLOCK * features,
        scratch=[vmem(tokens // BLOCK, H // PAIR, PAIR * HD, PAIR * HD, dtype=BF16)],
    )[0]


def turned_kernel(first, heads, ready, where, a_ref, b_ref, c_ref, *refs):
    if ready:
        ready_ref, out_ref, far_ref, sem = refs[-4:]
        copy = pltpu.make_async_copy(ready_ref, far_ref, sem)
        copy.start()
    else:
        out_ref = refs[-1]
    mask = triangle(CUT, True)

    def step(block, head):
        cols = head_cols(head)
        sums = attend(block, cols, a_ref, b_ref, c_ref, mask, True)
        for i, value in enumerate(sums):
            out_ref[block_part(block, i, 1), cols] = value

    over_units(a_ref.shape[0] // BLOCK, step, first, heads)
    if ready:
        copy.wait()


def turned_part(first, heads, a, b, c, made=(), ready=()):
    tokens, features = a.shape
    return call(
        functools.partial(turned_kernel, first, heads, len(ready)),
        [vmem(tokens, features)] + [jax.ShapeDtypeStruct(r.shape, r.dtype) for r in ready],
        [a, b, c, *made, *ready],
        4 * tokens * BLOCK * heads * HD,
        scratch=[pltpu.SemaphoreType.DMA(())] * len(ready),
        far_out=(1,) if ready else (),
        aliases={3: 0} if made else None,
    )


def final_kernel(slots, where, lk_ref, lv_ref, k_ref, v_ref, *refs):
    count = len(slots)
    carried, later = refs[:count], refs[count : 2 * count]
    gk_far, gv_far, gk_ref, gv_ref, sems = refs[-5:]
    copies = []
    for i, slot in enumerate(slots):
        for lane, share, head in heads_of(slot, where):
            cols, at = head_cols(head), len(copies) // 2
            for block in range(k_ref.shape[0] // BLOCK):
                rows = pl.ds(block * BLOCK, BLOCK)
                state = (carried[i][lane, share] + later[i][block, lane, share]).astype(BF16)
                grad_k = lk_ref[rows, cols] + mm(v_ref[rows, cols], state, 1, 1)
                grad_v = lv_ref[rows, cols] + mm(k_ref[rows, cols], state, 1, 0)
                gk_ref[at, rows, :], gv_ref[at, rows, :] = grad_k.astype(BF16), grad_v.astype(BF16)
            for j, (source, target) in enumerate(((gk_ref, gk_far), (gv_ref, gv_far))):
                copy = pltpu.make_async_copy(source.at[at], target.at[:, cols], sems.at[at, j])
                copy.start()
                copies.append(copy)
    for copy in copies:
        copy.wait()


def final_part(slots, local_k, local_v, keys, values, carried, later, made=()):
    tokens, features = keys.shape
    heads = len(slots) * LANES * SHARE
    args = [local_k, local_v, keys, values]
    args += [carried[o] for o in slots] + [later[o] for o in slots]
    places = range(len(args), len(args) + len(made))
    return call(
        functools.partial(final_kernel, slots),
        [jax.ShapeDtypeStruct((tokens, features), BF16)] * 2,
        [*args, *made],
        4 * tokens * heads * HD * HD,
        scratch=[vmem(heads, tokens, HD, dtype=BF16)] * 2 + [pltpu.SemaphoreType.DMA((heads, 2))],
        far_in=places,
        far_out=(0, 1),
        grant=12,
        aliases={place: i for i, place in enumerate(places)},
    )


def moved(value, move):
    groups, shards = lax.axis_size("grp"), lax.axis_size("seq")
    pairs = []
    for g in range(groups):
        for s in range(shards):
            to_g, to_s = move(g, s)
            pairs.append((g * shards + s, to_g * shards + to_s))
    return lax.ppermute(value, AXES, pairs)


def sum_kernel(where, *refs):
    held, (mine_ref, rest_ref) = refs[:QUAD], refs[QUAD:]
    for lane, out in enumerate((mine_ref, rest_ref)):
        out[...] = (held[0][lane] + held[1][lane]) + (held[2][lane] + held[3][lane])


def both_kernel(where, mine_ref, other_ref, both_ref):
    both_ref[...] = mine_ref[...] + other_ref[...]


def before(a, b, reverse):
    return a > b if reverse else a < b


def base_kernel(near_shifts, far_shifts, counts, reverse, where, mine_ref, other_ref, *refs):
    refs = list(refs)
    lane, row, far_row = where[0], where[2], where[3]
    takes = lane == (0 if reverse else 1)
    sum_mine = jnp.where(takes, other_ref[...], 0.0)
    sum_other = jnp.where(takes, 0.0, mine_ref[...])
    near_mine = [refs.pop(0) for _ in near_shifts]
    near_other = [refs.pop(0) for _ in near_shifts]
    for df, mine, other in zip(near_shifts, near_mine, near_other):
        near_by = before(lax.rem(far_row - df + counts[1], counts[1]), far_row, reverse)
        mine, other = mine[...], other[...]
        sum_mine += jnp.where(near_by, mine, 0.0) + jnp.where(takes, other, 0.0)
        sum_other += jnp.where(near_by, other, 0.0) + jnp.where(takes, 0.0, mine)
    for dr, _ in far_shifts:
        source = lax.rem(row - dr + counts[0], counts[0])
        add = jnp.where(before(source, row, reverse), refs.pop(0)[...], 0.0)
        sum_mine, sum_other = sum_mine + add, sum_other + add
    refs[0][...], refs[1][...] = sum_mine, sum_other


def back_sum_kernel(reverse, where, mine_ref, other_ref, *refs):
    held, back = refs[:QUAD], refs[QUAD:]
    quad = where[1]
    for lane, base in enumerate((mine_ref, other_ref)):
        for o in range(QUAD):
            value = base[...]
            for i in range(QUAD):
                if i != o:
                    near_by = before(quad ^ i, quad ^ o, reverse)
                    value += jnp.where(near_by, held[i][lane], 0.0)
            back[o][lane] = value


def far_shifts_of(counts):
    shifts = [(dr, df) for dr in range(1, counts[0]) for df in range(counts[1])]
    return sorted(shifts, key=lambda shift: -sum(shift))


def carry(first, rest, reverse):
    counts = lax.axis_size("grp") // LANES, lax.axis_size("seq") // QUAD
    one, two = vmem(SHARE, HD, HD), vmem(LANES, SHARE, HD, HD)

    def swap_quad(o):
        return lambda g, s: (g, s ^ o)

    def swap_lane(g, s):
        return g ^ 1, s

    def shift(dr, df):
        return lambda g, s: (
            (g // LANES + dr) % counts[0] * LANES + g % LANES,
            (s // QUAD + df) % counts[1] * QUAD + s % QUAD,
        )

    held, inside = [None] * QUAD, [None] * QUAD
    held[ORDER[0]], inside[ORDER[0]] = first
    held[ORDER[0]] = moved(held[ORDER[0]], swap_quad(ORDER[0]))
    sent = slot_totals(ORDER[1:-1], reverse, *rest)
    rest = {**sent, **slot_totals(ORDER[-1:], reverse, *rest)}
    for o in ORDER[1:]:
        held[o], inside[o] = rest[o]
        if o:
            held[o] = moved(held[o], swap_quad(o))
    mine, rest = call(sum_kernel, [one, one], [*held], 1000, grant=2)
    near_shifts, far_shifts = range(1, counts[1]), far_shifts_of(counts)
    came_mine, came_other, came_both = [], [], []
    for df in near_shifts:
        came_mine.append(moved(mine, shift(0, df)))
    other = moved(rest, swap_lane)
    for df in near_shifts:
        came_other.append(moved(other, shift(0, df)))
    both = call(both_kernel, [one], [mine, other], 1000, grant=2)[0]
    for dr, df in far_shifts:
        came_both.append(moved(both, shift(dr, df)))
    kernel = functools.partial(base_kernel, near_shifts, far_shifts, counts, reverse)
    args = [mine, other, *came_mine, *came_other, *came_both]
    sum_mine, sum_other = call(kernel, [one, one], args, 1000, grant=2)
    other = moved(sum_other, swap_lane)
    kernel = functools.partial(back_sum_kernel, reverse)
    back = call(kernel, [two] * QUAD, [sum_mine, other, *held], 1000, grant=2)
    result = [back[0]] + [None] * (QUAD - 1)
    for o in ORDER[:-1]:
        result[o] = moved(back[o], swap_quad(o))
    return result, inside


def body(queries, key_rows, value_rows, norm_gain, cotangent):
    gain = norm_gain[None, :]
    first = first_totals(ORDER[0], key_rows, value_rows)
    keys, values = near(key_rows), near(value_rows)
    piece, *first = first
    piece, queries, cotangent = lax.optimization_barrier((piece, queries, cotangent))
    first, queries, cotangent = [piece, *first], near(queries), near(cotangent)
    carried, inside = carry(first, (keys, values), False)
    attended = local_part(queries, keys, values)
    scores = turned_scores(keys, queries)
    priors, sums = [None] * QUAD, []
    for o in EARLY:
        attended, *sums, priors[o] = attended_slot(
            o, carried[o], inside[o], attended, queries, cotangent, gain, sums
        )
    late = [o for o in ORDER if o not in EARLY]
    normed, grads, late_priors, first = norm(
        late, carried, inside, attended, queries, cotangent, gain, sums
    )
    for o, prior in zip(late, late_priors):
        priors[o] = prior
    carried, later = carry(first, (queries, grads), True)
    local_v, normed = value_part(scores, grads, normed)
    local_k = turned_part(0, AHEAD, values, grads, queries)
    grad_q = query_part(grads, values, keys, priors)
    local_k, grad_q = turned_part(AHEAD, H - AHEAD, values, grads, queries, local_k, [grad_q])
    args = local_k, local_v, keys, values, carried, later
    made = final_part((0,) + ORDER[:1], *args)
    grad_k, grad_v = final_part(ORDER[1:-1], *args, made)
    return normed, grad_q, grad_k, grad_v


def solution(mesh):
    rows = P(AXES, None)
    return jax.shard_map(
        body,
        mesh=mesh,
        in_specs=(rows, rows, rows, P(), rows),
        out_specs=(rows, rows, rows, rows),
        check_vma=False,
    )
```
